32 devices in a mesh: row: 8 (over z, y), col: 4 (over x, core).
Axes of the slice: x: 2, y: 2, z: 4, core: 2. Of those that a mesh axis runs over, the one named last changes fastest.
Arguments:
- acts: bfloat16 [1024, 3072], P('row', 'col'), may hold values from -6 to 6
- grads: bfloat16 [1024, 3072], P('col', 'row'), may hold values from -0.19921875 to 0.19921875
- next_acts: bfloat16 [256, 3072], P('row', 'col'), may hold values from -6 to 6
- weight: bfloat16 [3072, 3072], P('row', 'col'), may hold values from -0.109375 to 0.109375
- moment: float32 [3072, 3072], P('row', 'col'), may hold values from -6 to 6
- second: float32 [3072, 3072], P('row', 'col'), may hold values from 0.05 to 5
- left_bank: bfloat16 [4, 384, 384], replicated, may hold values from -1 to 1, as said below
- right_bank: bfloat16 [4, 768, 768], P(None, 'row'), may hold values from -1 to 1, as said below
- left_index: int32 [8, 4], P('row', 'col'), may hold values from 0 to 3
- right_index: int32 [8, 4], P('row', 'col'), may hold values from 0 to 3
Outputs:
- update: bfloat16 [3072, 3072], P('row', 'col')
- next_out: bfloat16 [256, 3072], P('col', 'row')
The draws below stay inside these ranges and needn't reach their ends.
Inputs may be any that keep to these rules, and one draw needn't show every extreme that they name: `left_bank`: each basis is an orthogonal matrix rounded to bfloat16. `right_bank`: each basis is an orthogonal matrix rounded to bfloat16.
All inputs are finite; a program needn't handle non-finite values.
Results may differ from the reference program's by a relative error of at most 0.008.
Values may be sent and summed in bfloat16 or wider, within the bound.
A program may use at most 64 MiB of HBM per device.

```python
import math
import jax
import jax.numpy as jnp
from jax import lax

BO = 384
BI = 768
BANK = 4
TOKENS = 1024
NEXT = 256
D_OUT = 3072
D_IN = 3072
N_ROW = 8
N_COL = 4


def orthogonal_bank(key, count, order):
    normals = jax.random.normal(key, (count, order, order), jnp.float32)
    factors = jax.vmap(lambda matrix: jnp.linalg.qr(matrix)[0])(normals)
    return factors.astype(jnp.bfloat16)


def draw_left_bank(key, part):
    return orthogonal_bank(jax.random.fold_in(key, 11), BANK, BO)


def draw_right_bank(key, part):
    return orthogonal_bank(jax.random.fold_in(key, 23), BANK, BI)


def plant(values, stream_key, least, top_value):
    longest = values.shape.index(max(values.shape))
    spots = []
    for shift in (0, 1):
        where = [jax.random.randint(jax.random.fold_in(stream_key, axis), (), 0, length) for axis, length in enumerate(values.shape)]
        where[longest] = (where[longest] + shift) % values.shape[longest]
        spots.append(tuple(where))
    return values.at[spots[0]].set(least).at[spots[1]].set(top_value)


def block_scale(key, dims, split, least, top_value):
    loudness, own = 1.0, jax.random.fold_in(key, 6)
    for axis_at, shards_of in split:
        draws = jnp.exp(jax.random.uniform(jax.random.fold_in(own, axis_at), (shards_of,), jnp.float32, least / len(split), top_value / len(split)))
        loudness = loudness * jnp.repeat(draws, dims[axis_at] // shards_of).reshape([-1 if axis == axis_at else 1 for axis in range(len(dims))])
    return loudness


def normal_values(rng, extent, deviation, reach, cuts=(), dtype=jnp.bfloat16):
    drawn = jax.random.normal(rng, extent, jnp.float32) * deviation
    if len(cuts) > 0:
        drawn = block_scale(rng, extent, cuts, -0.22, 0.18) * drawn
    return jnp.clip(drawn, min=-reach, max=reach).astype(dtype)


def setup_inputs(seed: int = 0) -> dict:
    streams_of = jax.random.split(jax.random.key(seed), 11)
    return {
        "acts": normal_values(streams_of[0], (TOKENS, D_IN), 1.0, 6.0, ((0, 8), (1, 4))),
        "grads": normal_values(streams_of[1], (TOKENS, D_OUT), 0.03, 0.19921875, ((0, 4), (1, 8))),
        "next_acts": normal_values(streams_of[2], (NEXT, D_IN), 1.0, 6.0, ((0, 8), (1, 4))),
        "weight": normal_values(streams_of[3], (D_OUT, D_IN), D_IN ** -0.5, 0.109375, ((0, 8), (1, 4))),
        "moment": normal_values(streams_of[4], (D_OUT, D_IN), 1.0, 6.0, ((0, 8), (1, 4)), jnp.float32),
        "second": jnp.clip(jnp.exp(math.log(5.0) - 4.6051702 * jax.random.uniform(streams_of[5], (D_OUT, D_IN), jnp.float32) ** block_scale(streams_of[5], (D_OUT, D_IN), ((0, 8), (1, 4)), -0.2, 0.2)), 0.05, 5.0),
        "left_bank": draw_left_bank(jax.random.fold_in(streams_of[10], 71), 0),
        "right_bank": draw_right_bank(jax.random.fold_in(streams_of[10], 71), 0),
        "left_index": plant(jax.random.randint(streams_of[8], (N_ROW, N_COL), 0, BANK), jax.random.fold_in(streams_of[8], 1), 0, BANK - 1).astype(jnp.int32),
        "right_index": plant(jax.random.randint(streams_of[9], (N_ROW, N_COL), 0, BANK), jax.random.fold_in(streams_of[9], 1), 0, BANK - 1).astype(jnp.int32),
    }


HIGH = lax.Precision.HIGHEST

def to_blocks(array):
    return array.reshape(N_ROW, BO, N_COL, BI).transpose(0, 2, 1, 3).reshape(N_ROW * N_COL, BO, BI)

def from_blocks(array):
    return array.reshape(N_ROW, N_COL, BO, BI).transpose(0, 2, 1, 3).reshape(N_ROW * BO, N_COL * BI)

def reference(acts, grads, next_acts, weight, moment, second, left_bank, right_bank, left_index, right_index):
    f32 = jnp.float32
    gradient = jnp.dot(grads.astype(f32).T, acts.astype(f32), precision=HIGH).astype(jnp.bfloat16)

    def one_block(items):
        grad_block, weight_block, moment_block, second_block, left_pick, right_pick = items
        left_basis = lax.dynamic_index_in_dim(left_bank, left_pick, 0, keepdims=False).astype(f32)
        right_basis = lax.dynamic_index_in_dim(right_bank, right_pick, 0, keepdims=False).astype(f32)
        half = jnp.dot(left_basis.T, grad_block.astype(f32), precision=HIGH).astype(jnp.bfloat16)
        rotated = jnp.dot(half.astype(f32), right_basis, precision=HIGH)
        new_moment = 0.8 * moment_block + 0.2 * rotated
        new_second = 0.9 * second_block + 0.1 * rotated * rotated
        scaled = (new_moment / (jnp.sqrt(new_second) + 1e-08)).astype(jnp.bfloat16)
        back = jnp.dot(left_basis, scaled.astype(f32), precision=HIGH).astype(jnp.bfloat16)
        update_full = jnp.dot(back.astype(f32), right_basis.T, precision=HIGH)
        new_weight = (weight_block.astype(f32) - 0.001 * update_full).astype(jnp.bfloat16)
        return (update_full.astype(jnp.bfloat16), new_weight)
    updates, weights = lax.map(one_block, (to_blocks(gradient), to_blocks(weight), to_blocks(moment), to_blocks(second), left_index.reshape(-1).astype(jnp.int32), right_index.reshape(-1).astype(jnp.int32)))
    update = from_blocks(updates)
    new_weight = from_blocks(weights)
    next_out = jnp.dot(next_acts.astype(f32), new_weight.astype(f32).T, precision=HIGH).astype(jnp.bfloat16)
    return (update, next_out)
```

```python
import functools

import jax
import jax.numpy as jnp
from jax import lax
from jax.experimental import pallas as pl
from jax.experimental.pallas import tpu as pltpu
from jax.sharding import PartitionSpec as P

F32 = jnp.float32
BF16 = jnp.bfloat16
MESH = pl.DeviceIdType.MESH


def flip(value, bits, size):
    out, place = 0, 1
    while place < size:
        bit = (value // place) % 2
        out = out + place * ((1 - bit) if (bits // place) % 2 else bit)
        place *= 2
    return out


def as_matrix(value):
    cols = value.shape[-1]
    if value.shape[-2] % 16:
        return value.astype(F32).reshape(-1, cols).astype(BF16)
    return value.reshape(-1, cols)


def kernel(
    nz, nc,
    acts, grads, nxt, weight, moment, second, left_bank, right_bank, left_index, right_index,
    update, out,
    afull, gfull, gturn, nfull, wbuf, mbuf, sbuf, lbuf, lturn, bz, sel, rbuf,
    my_pick, picks, picks_smem, gacc, half, back, part, rsend, rrecv, ubuf, obuf,
    local, a_s, a_r, ay_s, ay_r, ad_s, n_s, n_r, ny_s, ny_r, nd_s, b_s, b_r,
    g_s, g_r, p_s, p_r, s_s, s_r, own_s, r_s, r_r,
):
    row, col = lax.axis_index("row"), lax.axis_index("col")
    z, y = row // 2, row % 2
    quad, q = col // 4, col % 4
    x, k = q // 2, q % 2
    tok = acts.shape[0]
    ntok = nxt.shape[0]
    gtok = grads.shape[0]
    width = acts.shape[1]
    lanes = width // 2
    slot = y * 4 + q
    my_lanes = pl.ds(pl.multiple_of(x * lanes, 128), lanes)

    def remote(src, dst, ss, rs, device):
        return pltpu.make_async_remote_copy(
            src_ref=src, dst_ref=dst, send_sem=ss, recv_sem=rs,
            device_id=device, device_id_type=MESH,
        )

    plane = [
        (dy * 4 + dq, 2 * z + ((1 - y) if dy else y), quad * 4 + flip(q, dq, 4),
         ((1 - y) if dy else y) * 4 + flip(q, dq, 4))
        for dy in range(2) for dq in range(4) if dy or dq
    ]
    col_peers = [(d, flip(col, d, nc)) for d in range(1, nc)]
    far_cols = [peer for d, peer in col_peers if d >= 4]
    mate = (2 * z + 1 - y, col)
    up, down = (2 * (z + 1) + y, col), (2 * (z - 1) + y, col)
    has_up, has_down = z < nz - 1, z > 0
    holds = z % 2 == k

    loads = [
        (acts, afull.at[z, y]), (nxt, nfull.at[z, y]),
        (grads, gfull.at[pl.ds(pl.multiple_of(col * gtok, gtok), gtok)]),
        (weight, wbuf), (moment, mbuf), (second, sbuf), (left_bank, lbuf),
    ]
    loads = [pltpu.make_async_copy(s, d, local.at[i]) for i, (s, d) in enumerate(loads)]
    own_bank = pltpu.make_async_copy(
        right_bank.at[:, :, my_lanes], bz.at[z // 2], local.at[7]
    )

    barrier = pltpu.get_barrier_semaphore()
    friends = [(r, c) for _, r, c, _ in plane] + [(row, c) for c in far_cols]
    for friend in friends:
        pl.semaphore_signal(barrier, inc=1, device_id=friend, device_id_type=MESH)
    for there, friend in ((has_up, up), (has_down, down)):
        @pl.when(there)
        def _(friend=friend):
            pl.semaphore_signal(barrier, inc=1, device_id=friend, device_id_type=MESH)

    @pl.when(holds)
    def _():
        own_bank.start()

    for load in loads:
        load.start()

    head = lax.broadcasted_iota(jnp.int32, my_pick.shape, 0) == 0
    my_pick[...] = jnp.where(
        head, jnp.broadcast_to(right_index[...], my_pick.shape),
        jnp.broadcast_to(left_index[...], my_pick.shape),
    )
    picks[slot] = my_pick[...]
    pl.semaphore_wait(
        barrier, len(friends) + jnp.where(has_up, 1, 0) + jnp.where(has_down, 1, 0)
    )

    sends, guards, handed = [], [], []

    def go(copy):
        copy.start()
        sends.append(copy)

    def guarded(cond, copy):
        @pl.when(cond)
        def _():
            copy.start()

        guards.append((cond, copy))

    def take(valid, copy):
        @pl.when(valid)
        def _():
            copy.wait_recv()

    def bank_copy(src, zs, ss, device):
        return remote(src, bz.at[zs // 2], ss, b_r.at[zs // 2], device)

    def both_ways(make, mine):
        guarded(has_up & mine, make(0, up))
        guarded(has_down & mine, make(1, down))

    yes = z >= 0

    def line(full, src, zs, ss, rs, to):
        return remote(src, full.at[zs, y], ss, rs.at[zs], to)

    def across(full, src, zs, ss, rs):
        return remote(src, full.at[zs, y], ss, rs.at[zs], mate)

    for e, r, c, _ in plane:
        go(remote(my_pick, picks.at[slot], p_s.at[e], p_r.at[slot], (r, c)))
    both_ways(lambda i, to: line(afull, acts, z, a_s.at[nz + i], a_r, to), yes)
    go(across(afull, acts, z, ay_s.at[z], ay_r))
    for d, c in col_peers:
        go(remote(grads, gfull.at[pl.ds(pl.multiple_of(col * gtok, gtok), gtok)],
                  g_s.at[d], g_r.at[col], (row, c)))
    bank_src = right_bank.at[:, :, my_lanes]
    both_ways(lambda i, to: bank_copy(bank_src, z, b_s.at[nz + i], to), holds)

    for e, r, c, s in plane:
        remote(my_pick, picks.at[s], p_s.at[e], p_r.at[s], (r, c)).wait_recv()
    to_smem = pltpu.make_async_copy(picks, picks_smem, local.at[8])
    to_smem.start()
    to_smem.wait()

    def place(zs, slot_from):
        ys, qs = slot_from // 4, slot_from % 4
        at = pl.ds(pl.multiple_of((qs // 2) * lanes, 128), lanes)
        return rbuf.at[zs // 2, qs % 2, ys, :, at]

    def plane_copy(zs, e, s, device):
        i = zs // 2
        return remote(sel.at[i, e], place(zs, s), s_s.at[i, e], s_r.at[i, s], device)

    def own_copy(zs):
        return pltpu.make_async_copy(sel.at[zs // 2, 0], place(zs, slot), own_s.at[zs // 2])

    def hand_out(zs, valid):
        @pl.when(valid)
        def _():
            for e, s in [(0, slot)] + [(e, s) for e, _, _, s in plane]:
                pick = picks_smem[s, 0, 0]
                piece = bz[zs // 2, 0]
                for b in range(1, bz.shape[1]):
                    piece = jnp.where(pick == b, bz[zs // 2, b], piece)
                sel[zs // 2, e] = piece
            own_copy(zs).start()
            for e, r, c, _ in plane:
                plane_copy(zs, e, slot, (r, c)).start()

        handed.append((zs, valid))

    @pl.when(holds)
    def _():
        own_bank.wait()

    hand_out(z, holds)
    go(across(nfull, nxt, z, ny_s.at[z], ny_r))

    def arrivals(hop):
        return [
            (lax.rem(zs + nz, nz), valid, on, to)
            for zs, valid, on, to in ((z - hop, z >= hop, has_up, up),
                                      (z + hop, z + hop < nz, has_down, down))
        ]

    def pass_bank(hop):
        for zs, valid, on, to in arrivals(hop):
            valid = valid & (zs % 2 == k)
            copy = bank_copy(bz.at[zs // 2], zs, b_s.at[zs], to)
            take(valid, copy)
            if hop < nz - 1:
                guarded(valid & on, copy)
            hand_out(zs, valid)

    def pass_acts(hop):
        for zs, valid, on, to in arrivals(hop):
            copy = line(afull, afull.at[zs, y], zs, a_s.at[zs], a_r, to)
            take(valid, copy)
            if hop < nz - 1:
                guarded(valid & on, copy)
            if hop > 1:
                guarded(valid, across(afull, afull.at[zs, y], zs, ay_s.at[zs], ay_r))

    def pass_next(hop, inner):
        for zs, valid, on, to in arrivals(hop):
            valid = valid & (on if inner else jnp.logical_not(on))
            copy = line(nfull, nfull.at[zs, y], zs, n_s.at[zs], n_r, to)
            take(valid, copy)
            if inner and hop < nz - 1:
                guarded(valid, copy)
            if hop > 1:
                guarded(valid, across(nfull, nfull.at[zs, y], zs, ny_s.at[zs], ny_r))

    def twice(full, zs, ss, rs, i, to):
        other = full.at[zs, 1 - y]
        return remote(other, other, ss.at[i], rs.at[zs], to)

    def take_other(full, zs, ss, rs):
        remote(full.at[zs, 1 - y], full.at[zs, 1 - y], ss.at[0], rs.at[zs], mate).wait_recv()

    for hop in range(1, nz - 1):
        pass_acts(hop)
        pass_bank(hop)

    take_other(afull, z, ay_s, ay_r)
    both_ways(lambda i, to: twice(afull, z, ad_s, ay_r, i, to), yes)
    both_ways(lambda i, to: line(nfull, nxt, z, n_s.at[nz + i], n_r, to), yes)
    take_other(nfull, z, ny_s, ny_r)
    both_ways(lambda i, to: twice(nfull, z, nd_s, ny_r, i, to), yes)

    for i in (0, 2, 6):
        loads[i].wait()
    left_at = picks_smem[slot, 1, 0]
    lturn[...] = lbuf[left_at].T
    for d, c in col_peers:
        remote(grads, gfull.at[pl.ds(pl.multiple_of(c * gtok, gtok), gtok)],
               g_s.at[d], g_r.at[c], (row, c)).wait_recv()
    gturn[...] = gfull[...].T

    def gather(d):
        zs = flip(z, d, nz) if d else z
        if d:
            take_other(afull, zs, ay_s, ay_r)
        return jnp.dot(
            gturn[:, pl.ds(pl.multiple_of(zs * 2 * tok, 2 * tok), 2 * tok)],
            afull[zs].reshape(2 * tok, width), preferred_element_type=F32,
        )

    gacc[...] = gather(0)
    pass_acts(nz - 1)
    pass_bank(nz - 1)
    for hop in range(1, nz):
        pass_next(hop, True)
    for d in list(range(2, nz)) + [1]:
        gacc[...] += gather(d)
    half[...] = jnp.dot(
        lturn[...], gacc[...].astype(BF16), preferred_element_type=F32
    ).astype(BF16)

    for i in range(nz // 2):
        for e, r, c, s in plane:
            plane_copy(2 * i, e, s, (r, c)).wait_recv()
    for zs, valid in handed:
        @pl.when(valid)
        def _(zs=zs):
            own_copy(zs).wait()

    for i in (3, 4, 5):
        loads[i].wait()
    left = lbuf[left_at]
    step = 256 if width % 256 == 0 else width
    right = as_matrix(rbuf[...])
    for n in range(0, width, step):
        cut = slice(n, n + step)
        rotated = jnp.dot(half[...], right[:, cut], preferred_element_type=F32)
        new_moment = 0.8 * mbuf[:, cut] + 0.2 * rotated
        new_second = 0.9 * sbuf[:, cut] + 0.1 * rotated * rotated
        scaled = (new_moment / (jnp.sqrt(new_second) + 1e-08)).astype(BF16)
        back[:, cut] = jnp.dot(left, scaled, preferred_element_type=F32).astype(BF16)

    for hop in range(1, nz - 1):
        pass_next(hop, False)

    for n in range(0, width, step):
        cut = slice(n, n + step)
        full = lax.dot_general(
            back[...], right[cut, :], (((1,), (1,)), ((), ())), preferred_element_type=F32
        )
        ubuf[:, cut] = full.astype(BF16)
        half[:, cut] = (wbuf[:, cut].astype(F32) - 0.001 * full).astype(BF16)
    put = pltpu.make_async_copy(ubuf, update, local.at[3])
    put.start()

    pass_next(nz - 1, False)
    loads[1].wait()

    def to_owner(zs, c):
        return remote(rsend.at[zs], rrecv.at[col], r_s.at[zs], r_r.at[col], (row, c))

    for d in [0] + list(range(2, nz)) + [1]:
        zs = flip(z, d, nz) if d else z
        if d:
            take_other(nfull, zs, ny_s, ny_r)
        term = lax.dot_general(
            nfull[zs].reshape(2 * ntok, width), half[...],
            (((1,), (1,)), ((), ())), preferred_element_type=F32,
        )

        @pl.when(zs == col)
        def _():
            part[...] = term

        @pl.when(zs != col)
        def _():
            rsend[zs] = term.astype(BF16)
            to_owner(zs, zs).start()

        guards.append((zs != col, to_owner(zs, zs)))

    total = part[...]
    for d, c in col_peers:
        remote(rsend.at[c], rrecv.at[c], r_s.at[c], r_r.at[c], (row, c)).wait_recv()
        total = total + rrecv[c].astype(F32)
    obuf[...] = total.astype(BF16)
    put_out = pltpu.make_async_copy(obuf, out, local.at[4])
    put_out.start()

    for copy in sends:
        copy.wait_send()

    for cond, copy in guards:
        @pl.when(cond)
        def _(copy=copy):
            copy.wait_send()

    for zs, valid in handed:
        @pl.when(valid)
        def _(zs=zs):
            for e, r, c, _ in plane:
                plane_copy(zs, e, slot, (r, c)).wait_send()

    put.wait()
    put_out.wait()


def finish(update_in, out_in, update, out, ubuf, obuf, sems):
    rows = ubuf.shape[0] // 4
    gets, puts = [], []
    for i in range(4):
        cut = pl.ds(i * rows, rows)
        gets.append(pltpu.make_async_copy(update_in.at[cut], ubuf.at[cut], sems.at[i]))
        puts.append(pltpu.make_async_copy(ubuf.at[cut], update.at[cut], sems.at[5 + i]))
    gets.append(pltpu.make_async_copy(out_in, obuf, sems.at[4]))
    puts.append(pltpu.make_async_copy(obuf, out, sems.at[9]))
    for get in gets:
        get.start()
    for get, put in zip(gets, puts):
        get.wait()
        put.start()
    for put in puts:
        put.wait()


def per_device(
    acts, grads, next_acts, weight, moment, second, left_bank, right_bank, left_index, right_index,
    *, nr, nc,
):
    nz = nr // 2
    tok, width = acts.shape
    gtok, bo = grads.shape
    ntok = next_acts.shape[0]
    bank, rrows, _ = right_bank.shape
    lanes = width // 2
    share = nr * ntok // nc
    dma = pltpu.SemaphoreType.DMA
    anyspace = pl.BlockSpec(memory_space=pl.ANY)
    vmem = pl.BlockSpec(memory_space=pltpu.VMEM)
    update, out = pl.pallas_call(
        functools.partial(kernel, nz, nc),
        out_shape=(
            jax.ShapeDtypeStruct(weight.shape, BF16),
            jax.ShapeDtypeStruct((share, bo), BF16),
        ),
        in_specs=[anyspace] * 8 + [vmem] * 2,
        out_specs=(anyspace, anyspace),
        scratch_shapes=[
            pltpu.VMEM((nz, 2, tok, width), BF16),
            pltpu.VMEM((nc * gtok, bo), BF16),
            pltpu.VMEM((bo, nc * gtok), BF16),
            pltpu.VMEM((nz, 2, ntok, width), BF16),
            pltpu.VMEM(weight.shape, BF16),
            pltpu.VMEM(weight.shape, F32),
            pltpu.VMEM(weight.shape, F32),
            pltpu.VMEM(left_bank.shape, BF16),
            pltpu.VMEM(left_bank.shape[1:], BF16),
            pltpu.VMEM((nz // 2, bank, rrows, lanes), BF16),
            pltpu.VMEM((nz // 2, 8, rrows, lanes), BF16),
            pltpu.VMEM((nz // 2, 2, 2, rrows, width), BF16),
            pltpu.VMEM((8, 128), jnp.int32),
            pltpu.VMEM((8, 8, 128), jnp.int32),
            pltpu.SMEM((8, 8, 128), jnp.int32),
            pltpu.VMEM(weight.shape, F32),
            pltpu.VMEM(weight.shape, BF16),
            pltpu.VMEM(weight.shape, BF16),
            pltpu.VMEM((share, bo), F32),
            pltpu.VMEM((nz, share, bo), BF16),
            pltpu.VMEM((nc, share, bo), BF16),
            pltpu.VMEM(weight.shape, BF16),
            pltpu.VMEM((share, bo), BF16),
            dma((10,)),
            dma((nz + 2,)), dma((nz,)), dma((nz,)), dma((nz,)), dma((2,)),
            dma((nz + 2,)), dma((nz,)), dma((nz,)), dma((nz,)), dma((2,)),
            dma((nz + 2,)), dma((nz // 2,)),
            dma((nc,)), dma((nc,)),
            dma((8,)), dma((8,)), dma((nz // 2, 8)), dma((nz // 2, 8)), dma((nz // 2,)),
            dma((nz,)), dma((nc,)),
        ],
        compiler_params=pltpu.CompilerParams(
            collective_id=0, has_side_effects=True, vmem_limit_bytes=60 * 2**20,
        ),
    )(acts, grads, next_acts, weight, moment, second, left_bank, right_bank, left_index,
      right_index)
    return pl.pallas_call(
        finish,
        out_shape=(
            jax.ShapeDtypeStruct(weight.shape, BF16),
            jax.ShapeDtypeStruct((share, bo), BF16),
        ),
        in_specs=[anyspace] * 2,
        out_specs=(anyspace, anyspace),
        scratch_shapes=[
            pltpu.VMEM(weight.shape, BF16), pltpu.VMEM((share, bo), BF16), dma((10,)),
        ],
    )(update, out)


def solution(mesh):
    nr, nc = mesh.shape["row"], mesh.shape["col"]
    return jax.shard_map(
        functools.partial(per_device, nr=nr, nc=nc),
        mesh=mesh,
        in_specs=(
            P("row", "col"), P("col", "row"), P("row", "col"), P("row", "col"),
            P("row", "col"), P("row", "col"), P(), P(None, "row", None),
            P("row", "col"), P("row", "col"),
        ),
        out_specs=(P("row", "col"), P("col", "row")),
        check_vma=False,
    )
```

```python
import functools

import jax
import jax.numpy as jnp
from jax import lax
from jax.experimental import pallas as pl
from jax.experimental.pallas import tpu as pltpu
from jax.sharding import PartitionSpec as P

F32 = jnp.float32
BF16 = jnp.bfloat16
MESH = pl.DeviceIdType.MESH


def flip(value, bits, size):
    out, place = 0, 1
    while place < size:
        bit = (value // place) % 2
        out = out + place * ((1 - bit) if (bits // place) % 2 else bit)
        place *= 2
    return out


def as_matrix(value):
    cols = value.shape[-1]
    if value.shape[-2] % 16:
        return value.astype(F32).reshape(-1, cols).astype(BF16)
    return value.reshape(-1, cols)


def kernel(
    nz, nc,
    acts, grads, nxt, weight, moment, second, left_bank, right_bank, left_index, right_index,
    update, out,
    afull, gfull, gturn, nfull, wbuf, mbuf, sbuf, lbuf, lturn, bz, sel, rbuf,
    my_pick, picks, picks_smem, gacc, half, back, part, rsend, rrecv, ubuf, obuf,
    local, a_s, a_r, ay_s, ay_r, ad_s, ad_r, n_s, n_r, ny_s, ny_r, b_s, b_r,
    g_s, g_r, p_s, p_r, s_s, s_r, own_s, r_s, r_r,
):
    row, col = lax.axis_index("row"), lax.axis_index("col")
    z, y = row // 2, row % 2
    quad, q = col // 4, col % 4
    x, k = q // 2, q % 2
    tok = acts.shape[0]
    ntok = nxt.shape[0]
    gtok = grads.shape[0]
    width = acts.shape[1]
    lanes = width // 2
    slot = y * 4 + q
    my_lanes = pl.ds(pl.multiple_of(x * lanes, 128), lanes)

    def remote(src, dst, ss, rs, device):
        return pltpu.make_async_remote_copy(
            src_ref=src, dst_ref=dst, send_sem=ss, recv_sem=rs,
            device_id=device, device_id_type=MESH,
        )

    plane = [
        (dy * 4 + dq, 2 * z + ((1 - y) if dy else y), quad * 4 + flip(q, dq, 4),
         ((1 - y) if dy else y) * 4 + flip(q, dq, 4))
        for dy in range(2) for dq in range(4) if dy or dq
    ]
    col_peers = [(d, flip(col, d, nc)) for d in range(1, nc)]
    far_cols = [peer for d, peer in col_peers if d >= 4]
    mate = (2 * z + 1 - y, col)
    up, down = (2 * (z + 1) + y, col), (2 * (z - 1) + y, col)
    has_up, has_down = z < nz - 1, z > 0
    holds = z % 2 == k

    loads = [
        (acts, afull.at[z, y]), (nxt, nfull.at[z, y]),
        (grads, gfull.at[pl.ds(pl.multiple_of(col * gtok, gtok), gtok)]),
        (weight, wbuf), (moment, mbuf), (second, sbuf), (left_bank, lbuf),
    ]
    loads = [pltpu.make_async_copy(s, d, local.at[i]) for i, (s, d) in enumerate(loads)]
    own_bank = pltpu.make_async_copy(
        right_bank.at[:, :, my_lanes], bz.at[z // 2], local.at[7]
    )

    barrier = pltpu.get_barrier_semaphore()
    friends = [(r, c) for _, r, c, _ in plane] + [(row, c) for c in far_cols]
    for friend in friends:
        pl.semaphore_signal(barrier, inc=1, device_id=friend, device_id_type=MESH)
    for there, friend in ((has_up, up), (has_down, down)):
        @pl.when(there)
        def _(friend=friend):
            pl.semaphore_signal(barrier, inc=1, device_id=friend, device_id_type=MESH)

    @pl.when(holds)
    def _():
        own_bank.start()

    for load in loads:
        load.start()

    head = lax.broadcasted_iota(jnp.int32, my_pick.shape, 0) == 0
    my_pick[...] = jnp.where(
        head, jnp.broadcast_to(right_index[...], my_pick.shape),
        jnp.broadcast_to(left_index[...], my_pick.shape),
    )
    picks[slot] = my_pick[...]
    pl.semaphore_wait(
        barrier, len(friends) + jnp.where(has_up, 1, 0) + jnp.where(has_down, 1, 0)
    )

    sends, guards, handed = [], [], []

    def go(copy):
        copy.start()
        sends.append(copy)

    def guarded(cond, copy):
        @pl.when(cond)
        def _():
            copy.start()

        guards.append((cond, copy))

    def take(valid, copy):
        @pl.when(valid)
        def _():
            copy.wait_recv()

    def bank_copy(src, zs, ss, device):
        return remote(src, bz.at[zs // 2], ss, b_r.at[zs // 2], device)

    def both_ways(make, mine):
        guarded(has_up & mine, make(0, up))
        guarded(has_down & mine, make(1, down))

    yes = z >= 0
    early = tok // 2

    def line(full, src, zs, ss, rs, to):
        return remote(src, full.at[zs, y], ss, rs.at[zs], to)

    def at_end(zs):
        return (zs == 0) | (zs == nz - 1)

    for e, r, c, _ in plane:
        go(remote(my_pick, picks.at[slot], p_s.at[e], p_r.at[slot], (r, c)))
    bank_src = right_bank.at[:, :, my_lanes]
    both_ways(lambda i, to: bank_copy(bank_src, z, b_s.at[nz + i], to), holds)
    both_ways(lambda i, to: line(afull, acts, z, a_s.at[nz + i], a_r, to), yes)
    go(remote(acts, afull.at[z, y], ay_s.at[z], ay_r.at[z], mate))
    go(remote(nxt, nfull.at[z, y], ny_s.at[0], ny_r.at[0], mate))
    for d, c in col_peers:
        go(remote(grads, gfull.at[pl.ds(pl.multiple_of(col * gtok, gtok), gtok)],
                  g_s.at[d], g_r.at[col], (row, c)))

    for e, r, c, s in plane:
        remote(my_pick, picks.at[s], p_s.at[e], p_r.at[s], (r, c)).wait_recv()
    to_smem = pltpu.make_async_copy(picks, picks_smem, local.at[8])
    to_smem.start()
    to_smem.wait()

    def place(zs, slot_from):
        ys, qs = slot_from // 4, slot_from % 4
        at = pl.ds(pl.multiple_of((qs // 2) * lanes, 128), lanes)
        return rbuf.at[zs // 2, qs % 2, ys, :, at]

    def plane_copy(zs, e, s, device):
        i = zs // 2
        return remote(sel.at[i, e], place(zs, s), s_s.at[i, e], s_r.at[i, s], device)

    def own_copy(zs):
        return pltpu.make_async_copy(sel.at[zs // 2, 0], place(zs, slot), own_s.at[zs // 2])

    def hand_out(zs, valid):
        @pl.when(valid)
        def _():
            for e, s in [(0, slot)] + [(e, s) for e, _, _, s in plane]:
                pick = picks_smem[s, 0, 0]
                piece = bz[zs // 2, 0]
                for b in range(1, bz.shape[1]):
                    piece = jnp.where(pick == b, bz[zs // 2, b], piece)
                sel[zs // 2, e] = piece
            own_copy(zs).start()
            for e, r, c, _ in plane:
                plane_copy(zs, e, slot, (r, c)).start()

        handed.append((zs, valid))

    @pl.when(holds)
    def _():
        own_bank.wait()

    hand_out(z, holds)

    def arrivals(hop):
        return [
            (lax.rem(zs + nz, nz), valid, on, to)
            for zs, valid, on, to in ((z - hop, z >= hop, has_up, up),
                                      (z + hop, z + hop < nz, has_down, down))
        ]

    def pass_bank(hop):
        for zs, valid, on, to in arrivals(hop):
            valid = valid & (zs % 2 == k)
            copy = bank_copy(bz.at[zs // 2], zs, b_s.at[zs], to)
            take(valid, copy)
            if hop < nz - 1:
                guarded(valid & on, copy)
            hand_out(zs, valid)

    def across(zs, rows):
        piece = afull.at[zs, y, rows]
        return remote(piece, piece, ay_s.at[zs], ay_r.at[zs], mate)

    def pass_acts(hop):
        for zs, valid, on, to in arrivals(hop):
            copy = line(afull, afull.at[zs, y], zs, a_s.at[zs], a_r, to)
            take(valid, copy)
            if hop < nz - 1:
                guarded(valid & on, copy)
            guarded(valid & at_end(zs), across(zs, pl.ds(0, early)))
            guarded(valid & jnp.logical_not(at_end(zs)), across(zs, pl.ds(0, tok)))

    def rest_copy(zs, to):
        piece = afull.at[zs, 1 - y, pl.ds(early, tok - early)]
        return remote(piece, piece, ad_s.at[zs], ad_r.at[zs], to)

    def pass_rest(hop):
        for zs, valid, on, to in arrivals(hop):
            valid = valid & at_end(zs)
            copy = rest_copy(zs, to)
            take(valid, copy)
            if hop < nz - 1:
                guarded(valid & on, copy)

    def next_copy(zs, ss, to):
        return remote(nfull.at[zs], nfull.at[zs], ss, n_r.at[zs], to)

    def own_next(hop):
        guarded(z == hop, next_copy(z, n_s.at[nz], up))
        guarded(z == nz - 1 - hop, next_copy(z, n_s.at[nz + 1], down))

    def pass_next(hop, inner):
        for zs, valid, on, to in arrivals(hop):
            valid = valid & (on if inner else jnp.logical_not(on))
            copy = next_copy(zs, n_s.at[zs], to)
            take(valid, copy)
            if inner and hop < nz - 1:
                guarded(valid, copy)

    def take_acts(zs, rows):
        piece = afull.at[zs, 1 - y, rows]
        remote(piece, piece, ay_s.at[0], ay_r.at[zs], mate).wait_recv()

    def gather(d):
        zs = flip(z, d, nz) if d else z
        if d:
            @pl.when(at_end(zs))
            def _():
                take_acts(zs, pl.ds(0, early))

            @pl.when(jnp.logical_not(at_end(zs)))
            def _():
                take_acts(zs, pl.ds(0, tok))
        return jnp.dot(
            gturn[:, pl.ds(pl.multiple_of(zs * 2 * tok, 2 * tok), 2 * tok)],
            afull[zs].reshape(2 * tok, width), preferred_element_type=F32,
        )

    pass_bank(1)
    take_acts(z, pl.ds(0, tok))
    guarded(z == 0, rest_copy(z, up))
    guarded(z == nz - 1, rest_copy(z, down))
    loads[1].wait()
    remote(nxt, nfull.at[z, 1 - y], ny_s.at[0], ny_r.at[0], mate).wait_recv()
    own_next(0)
    pass_acts(1)
    if nz > 2:
        pass_bank(2)
        pass_rest(1)
        own_next(1)

    for i in (0, 2, 6):
        loads[i].wait()
    left_at = picks_smem[slot, 1, 0]
    lturn[...] = lbuf[left_at].T
    for d, c in col_peers:
        remote(grads, gfull.at[pl.ds(pl.multiple_of(c * gtok, gtok), gtok)],
               g_s.at[d], g_r.at[c], (row, c)).wait_recv()
    gturn[...] = gfull[...].T

    gacc[...] = gather(0)
    for hop in range(2, nz - 1):
        pass_acts(hop)
        pass_bank(hop + 1)
        pass_rest(hop)
        own_next(hop)
    for hop in range(1, nz - 1):
        pass_next(hop, True)
    pass_acts(nz - 1)
    for d in range(1, nz - 1):
        gacc[...] += gather(d)
    pass_rest(nz - 1)
    gacc[...] += gather(nz - 1)
    half[...] = jnp.dot(
        lturn[...], gacc[...].astype(BF16), preferred_element_type=F32
    ).astype(BF16)

    for i in range(nz // 2):
        for e, r, c, s in plane:
            plane_copy(2 * i, e, s, (r, c)).wait_recv()
    for zs, valid in handed:
        @pl.when(valid)
        def _(zs=zs):
            own_copy(zs).wait()

    for i in (3, 4, 5):
        loads[i].wait()
    left = lbuf[left_at]
    step = 256 if width % 256 == 0 else width
    right = as_matrix(rbuf[...])
    for n in range(0, width, step):
        cut = slice(n, n + step)
        rotated = jnp.dot(half[...], right[:, cut], preferred_element_type=F32)
        new_moment = 0.8 * mbuf[:, cut] + 0.2 * rotated
        new_second = 0.9 * sbuf[:, cut] + 0.1 * rotated * rotated
        scaled = (new_moment / (jnp.sqrt(new_second) + 1e-08)).astype(BF16)
        back[:, cut] = jnp.dot(left, scaled, preferred_element_type=F32).astype(BF16)

    for n in range(0, width, step):
        cut = slice(n, n + step)
        full = lax.dot_general(
            back[...], right[cut, :], (((1,), (1,)), ((), ())), preferred_element_type=F32
        )
        update[:, cut] = full.astype(BF16)
        half[:, cut] = (wbuf[:, cut].astype(F32) - 0.001 * full).astype(BF16)

    for hop in range(1, nz):
        pass_next(hop, False)

    def to_owner(zs, c):
        return remote(rsend.at[zs], rrecv.at[col], r_s.at[zs], r_r.at[col], (row, c))

    for d in range(nz):
        zs = flip(z, d, nz) if d else z
        term = lax.dot_general(
            nfull[zs].reshape(2 * ntok, width), half[...],
            (((1,), (1,)), ((), ())), preferred_element_type=F32,
        )

        @pl.when(zs == col)
        def _():
            part[...] = term

        @pl.when(zs != col)
        def _():
            rsend[zs] = term.astype(BF16)
            to_owner(zs, zs).start()

        guards.append((zs != col, to_owner(zs, zs)))

    total = part[...]
    for d, c in col_peers:
        remote(rsend.at[c], rrecv.at[c], r_s.at[c], r_r.at[c], (row, c)).wait_recv()
        total = total + rrecv[c].astype(F32)
    out[...] = total.astype(BF16)

    for copy in sends:
        copy.wait_send()

    for cond, copy in guards:
        @pl.when(cond)
        def _(copy=copy):
            copy.wait_send()

    for zs, valid in handed:
        @pl.when(valid)
        def _(zs=zs):
            for e, r, c, _ in plane:
                plane_copy(zs, e, slot, (r, c)).wait_send()


def finish(update_in, out_in, update, out, sems):
    puts = [
        pltpu.make_async_copy(update_in, update, sems.at[0]),
        pltpu.make_async_copy(out_in, out, sems.at[1]),
    ]
    for put in puts:
        put.start()
    for put in puts:
        put.wait()


def per_device(
    acts, grads, next_acts, weight, moment, second, left_bank, right_bank, left_index, right_index,
    *, nr, nc,
):
    nz = nr // 2
    tok, width = acts.shape
    gtok, bo = grads.shape
    ntok = next_acts.shape[0]
    bank, rrows, _ = right_bank.shape
    lanes = width // 2
    share = nr * ntok // nc
    dma = pltpu.SemaphoreType.DMA
    anyspace = pl.BlockSpec(memory_space=pl.ANY)
    acts, grads, next_acts, weight, moment, second, left_bank, right_bank = [
        pltpu.with_memory_space_constraint(a, pltpu.HBM)
        for a in (acts, grads, next_acts, weight, moment, second, left_bank, right_bank)
    ]
    vmem = pl.BlockSpec(memory_space=pltpu.VMEM)
    update, out = pl.pallas_call(
        functools.partial(kernel, nz, nc),
        out_shape=(
            pltpu.VMEM(weight.shape, BF16),
            pltpu.VMEM((share, bo), BF16),
        ),
        in_specs=[anyspace] * 8 + [vmem] * 2,
        out_specs=(vmem, vmem),
        scratch_shapes=[
            pltpu.VMEM((nz, 2, tok, width), BF16),
            pltpu.VMEM((nc * gtok, bo), BF16),
            pltpu.VMEM((bo, nc * gtok), BF16),
            pltpu.VMEM((nz, 2, ntok, width), BF16),
            pltpu.VMEM(weight.shape, BF16),
            pltpu.VMEM(weight.shape, F32),
            pltpu.VMEM(weight.shape, F32),
            pltpu.VMEM(left_bank.shape, BF16),
            pltpu.VMEM(left_bank.shape[1:], BF16),
            pltpu.VMEM((nz // 2, bank, rrows, lanes), BF16),
            pltpu.VMEM((nz // 2, 8, rrows, lanes), BF16),
            pltpu.VMEM((nz // 2, 2, 2, rrows, width), BF16),
            pltpu.VMEM((8, 128), jnp.int32),
            pltpu.VMEM((8, 8, 128), jnp.int32),
            pltpu.SMEM((8, 8, 128), jnp.int32),
            pltpu.VMEM(weight.shape, F32),
            pltpu.VMEM(weight.shape, BF16),
            pltpu.VMEM(weight.shape, BF16),
            pltpu.VMEM((share, bo), F32),
            pltpu.VMEM((nz, share, bo), BF16),
            pltpu.VMEM((nc, share, bo), BF16),
            pltpu.VMEM(weight.shape, BF16),
            pltpu.VMEM((share, bo), BF16),
            dma((10,)),
            dma((nz + 2,)), dma((nz,)), dma((nz,)), dma((nz,)), dma((nz,)), dma((nz,)),
            dma((nz + 2,)), dma((nz,)), dma((1,)), dma((1,)),
            dma((nz + 2,)), dma((nz // 2,)),
            dma((nc,)), dma((nc,)),
            dma((8,)), dma((8,)), dma((nz // 2, 8)), dma((nz // 2, 8)), dma((nz // 2,)),
            dma((nz,)), dma((nc,)),
        ],
        compiler_params=pltpu.CompilerParams(
            collective_id=0, has_side_effects=True, vmem_limit_bytes=40 * 2**20,
        ),
    )(acts, grads, next_acts, weight, moment, second, left_bank, right_bank, left_index,
      right_index)
    update, out = [pltpu.with_memory_space_constraint(a, pltpu.VMEM) for a in (update, out)]
    return pl.pallas_call(
        finish,
        out_shape=(
            jax.ShapeDtypeStruct(weight.shape, BF16),
            jax.ShapeDtypeStruct((share, bo), BF16),
        ),
        in_specs=[vmem] * 2,
        out_specs=(anyspace, anyspace),
        scratch_shapes=[dma((2,))],
    )(update, out)


def solution(mesh):
    nr, nc = mesh.shape["row"], mesh.shape["col"]
    return jax.shard_map(
        functools.partial(per_device, nr=nr, nc=nc),
        mesh=mesh,
        in_specs=(
            P("row", "col"), P("col", "row"), P("row", "col"), P("row", "col"),
            P("row", "col"), P("row", "col"), P(), P(None, "row", None),
            P("row", "col"), P("row", "col"),
        ),
        out_specs=(P("row", "col"), P("col", "row")),
        check_vma=False,
    )
```

```python
import functools

import jax
import jax.numpy as jnp
from jax import lax
from jax.experimental import pallas as pl
from jax.experimental.pallas import tpu as pltpu
from jax.sharding import PartitionSpec as P

F32 = jnp.float32
BF16 = jnp.bfloat16
MESH = pl.DeviceIdType.MESH


def flip(value, bits, size):
    out, place = 0, 1
    while place < size:
        bit = (value // place) % 2
        out = out + place * ((1 - bit) if (bits // place) % 2 else bit)
        place *= 2
    return out


def as_matrix(value):
    cols = value.shape[-1]
    if value.shape[-2] % 16:
        return value.astype(F32).reshape(-1, cols).astype(BF16)
    return value.reshape(-1, cols)


def kernel(
    nz, nc,
    acts, grads, nxt, weight, moment, second, left_bank, right_bank, left_index, right_index,
    update, out,
    afull, gfull, gturn, nfull, wbuf, mbuf, sbuf, lbuf, bz, sel, rbuf,
    my_pick, picks, picks_smem, gacc, half, back, terms, rsend, rrecv, ubuf, obuf,
    local, a_s, a_r, ay_s, ay_r, ad_s, ad_r, n_s, n_r, ny_s, ny_r, b_s, b_r,
    g_s, g_r, p_s, p_r, s_s, s_r, own_s, r_s, r_r,
):
    row, col = lax.axis_index("row"), lax.axis_index("col")
    z, y = row // 2, row % 2
    quad, q = col // 4, col % 4
    x, k = q // 2, q % 2
    tok = acts.shape[0]
    ntok = nxt.shape[0]
    gtok = grads.shape[0]
    width = acts.shape[1]
    lanes = width // 2
    slot = y * 4 + q
    my_lanes = pl.ds(pl.multiple_of(x * lanes, 128), lanes)

    def remote(src, dst, ss, rs, device):
        return pltpu.make_async_remote_copy(
            src_ref=src, dst_ref=dst, send_sem=ss, recv_sem=rs,
            device_id=device, device_id_type=MESH,
        )

    plane = [
        (dy * 4 + dq, 2 * z + ((1 - y) if dy else y), quad * 4 + flip(q, dq, 4),
         ((1 - y) if dy else y) * 4 + flip(q, dq, 4))
        for dy in range(2) for dq in range(4) if dy or dq
    ]
    col_peers = [(d, flip(col, d, nc)) for d in range(1, nc)]
    far_cols = [peer for d, peer in col_peers if d >= 4]
    mate = (2 * z + 1 - y, col)
    up, down = (2 * (z + 1) + y, col), (2 * (z - 1) + y, col)
    has_up, has_down = z < nz - 1, z > 0
    holds = z % 2 == k

    loads = [
        (acts, afull.at[z, y]), (nxt, nfull.at[z, y]),
        (grads, gfull.at[pl.ds(pl.multiple_of(col * gtok, gtok), gtok)]),
        (weight, wbuf), (moment, mbuf), (second, sbuf), (left_bank, lbuf),
    ]
    loads = [pltpu.make_async_copy(s, d, local.at[i]) for i, (s, d) in enumerate(loads)]
    own_bank = pltpu.make_async_copy(
        right_bank.at[:, :, my_lanes], bz.at[z // 2], local.at[7]
    )

    barrier = pltpu.get_barrier_semaphore()
    friends = [(r, c) for _, r, c, _ in plane] + [(row, c) for c in far_cols]
    for friend in friends:
        pl.semaphore_signal(barrier, inc=1, device_id=friend, device_id_type=MESH)
    for there, friend in ((has_up, up), (has_down, down)):
        @pl.when(there)
        def _(friend=friend):
            pl.semaphore_signal(barrier, inc=1, device_id=friend, device_id_type=MESH)

    @pl.when(holds)
    def _():
        own_bank.start()

    for load in loads:
        load.start()

    head = lax.broadcasted_iota(jnp.int32, my_pick.shape, 0) == 0
    my_pick[...] = jnp.where(
        head, jnp.broadcast_to(right_index[...], my_pick.shape),
        jnp.broadcast_to(left_index[...], my_pick.shape),
    )
    picks[slot] = my_pick[...]
    pl.semaphore_wait(
        barrier, len(friends) + jnp.where(has_up, 1, 0) + jnp.where(has_down, 1, 0)
    )

    sends, guards, handed = [], [], []

    def go(copy):
        copy.start()
        sends.append(copy)

    def guarded(cond, copy):
        @pl.when(cond)
        def _():
            copy.start()

        guards.append((cond, copy))

    def take(valid, copy):
        @pl.when(valid)
        def _():
            copy.wait_recv()

    def bank_copy(src, zs, ss, device):
        return remote(src, bz.at[zs // 2], ss, b_r.at[zs // 2], device)

    def both_ways(make, mine):
        guarded(has_up & mine, make(0, up))
        guarded(has_down & mine, make(1, down))

    yes = z >= 0
    early = 3 * tok // 8

    def line(full, src, zs, ss, rs, to):
        return remote(src, full.at[zs, y], ss, rs.at[zs], to)

    def at_end(zs):
        return (zs == 0) | (zs == nz - 1)

    for e, r, c, _ in plane:
        go(remote(my_pick, picks.at[slot], p_s.at[e], p_r.at[slot], (r, c)))
    bank_src = right_bank.at[:, :, my_lanes]
    both_ways(lambda i, to: bank_copy(bank_src, z, b_s.at[nz + i], to), holds)
    both_ways(lambda i, to: line(afull, acts, z, a_s.at[nz + i], a_r, to), yes)
    go(remote(acts, afull.at[z, y], ay_s.at[z], ay_r.at[z], mate))
    go(remote(nxt, nfull.at[z, y], ny_s.at[0], ny_r.at[0], mate))
    for d, c in col_peers:
        go(remote(grads, gfull.at[pl.ds(pl.multiple_of(col * gtok, gtok), gtok)],
                  g_s.at[d], g_r.at[col], (row, c)))

    for e, r, c, s in plane:
        remote(my_pick, picks.at[s], p_s.at[e], p_r.at[s], (r, c)).wait_recv()
    to_smem = pltpu.make_async_copy(picks, picks_smem, local.at[8])
    to_smem.start()
    to_smem.wait()

    def place(zs, slot_from):
        ys, qs = slot_from // 4, slot_from % 4
        at = pl.ds(pl.multiple_of((qs // 2) * lanes, 128), lanes)
        return rbuf.at[zs // 2, qs % 2, ys, :, at]

    def plane_copy(zs, e, s, device):
        i = zs // 2
        return remote(sel.at[i, e], place(zs, s), s_s.at[i, e], s_r.at[i, s], device)

    def own_copy(zs):
        return pltpu.make_async_copy(sel.at[zs // 2, 0], place(zs, slot), own_s.at[zs // 2])

    def hand_out(zs, valid):
        @pl.when(valid)
        def _():
            for e, s in [(0, slot)] + [(e, s) for e, _, _, s in plane]:
                pick = picks_smem[s, 0, 0]
                piece = bz[zs // 2, 0]
                for b in range(1, bz.shape[1]):
                    piece = jnp.where(pick == b, bz[zs // 2, b], piece)
                sel[zs // 2, e] = piece
            own_copy(zs).start()
            for e, r, c, _ in plane:
                plane_copy(zs, e, slot, (r, c)).start()

        handed.append((zs, valid))

    @pl.when(holds)
    def _():
        own_bank.wait()

    hand_out(z, holds)

    def arrivals(hop):
        return [
            (lax.rem(zs + nz, nz), valid, on, to)
            for zs, valid, on, to in ((z - hop, z >= hop, has_up, up),
                                      (z + hop, z + hop < nz, has_down, down))
        ]

    def pass_bank(hop):
        for zs, valid, on, to in arrivals(hop):
            valid = valid & (zs % 2 == k)
            copy = bank_copy(bz.at[zs // 2], zs, b_s.at[zs], to)
            take(valid, copy)
            if hop < nz - 1:
                guarded(valid & on, copy)
            hand_out(zs, valid)

    def across(zs, rows):
        piece = afull.at[zs, y, rows]
        return remote(piece, piece, ay_s.at[zs], ay_r.at[zs], mate)

    def pass_acts(hop):
        for zs, valid, on, to in arrivals(hop):
            copy = line(afull, afull.at[zs, y], zs, a_s.at[zs], a_r, to)
            take(valid, copy)
            if hop < nz - 1:
                guarded(valid & on, copy)
            guarded(valid & at_end(zs), across(zs, pl.ds(0, early)))
            guarded(valid & jnp.logical_not(at_end(zs)), across(zs, pl.ds(0, tok)))

    def rest_copy(zs, to):
        piece = afull.at[zs, 1 - y, pl.ds(early, tok - early)]
        return remote(piece, piece, ad_s.at[zs], ad_r.at[zs], to)

    def pass_rest(hop):
        for zs, valid, on, to in arrivals(hop):
            valid = valid & at_end(zs)
            copy = rest_copy(zs, to)
            take(valid, copy)
            if hop < nz - 1:
                guarded(valid & on, copy)

    def next_copy(zs, ss, to):
        return remote(nfull.at[zs], nfull.at[zs], ss, n_r.at[zs], to)

    def own_next(hop):
        guarded(z == hop, next_copy(z, n_s.at[nz], up))
        guarded(z == nz - 1 - hop, next_copy(z, n_s.at[nz + 1], down))

    def pass_next(hop, inner):
        for zs, valid, on, to in arrivals(hop):
            valid = valid & (on if inner else jnp.logical_not(on))
            copy = next_copy(zs, n_s.at[zs], to)
            take(valid, copy)
            if inner and hop < nz - 1:
                guarded(valid, copy)

    def take_acts(zs, rows):
        piece = afull.at[zs, 1 - y, rows]
        remote(piece, piece, ay_s.at[0], ay_r.at[zs], mate).wait_recv()

    def gather(d):
        zs = flip(z, d, nz) if d else z
        if d:
            @pl.when(at_end(zs))
            def _():
                take_acts(zs, pl.ds(0, early))

            @pl.when(jnp.logical_not(at_end(zs)))
            def _():
                take_acts(zs, pl.ds(0, tok))
        return jnp.dot(
            gturn[:, pl.ds(pl.multiple_of(zs * 2 * tok, 2 * tok), 2 * tok)],
            afull[zs].reshape(2 * tok, width), preferred_element_type=F32,
        )

    pass_bank(1)
    take_acts(z, pl.ds(0, tok))
    guarded(z == 0, rest_copy(z, up))
    guarded(z == nz - 1, rest_copy(z, down))
    loads[1].wait()
    remote(nxt, nfull.at[z, 1 - y], ny_s.at[0], ny_r.at[0], mate).wait_recv()
    own_next(0)
    pass_acts(1)
    if nz > 2:
        pass_bank(2)
        pass_rest(1)
        own_next(1)

    for i in (0, 2, 6):
        loads[i].wait()
    left_at = picks_smem[slot, 1, 0]
    left = lbuf[left_at]
    for d, c in col_peers:
        remote(grads, gfull.at[pl.ds(pl.multiple_of(c * gtok, gtok), gtok)],
               g_s.at[d], g_r.at[c], (row, c)).wait_recv()
    gturn[...] = lax.dot_general(
        left, gfull[...], (((0,), (1,)), ((), ())), preferred_element_type=F32
    ).astype(BF16)

    gacc[...] = gather(0)
    for hop in range(2, nz - 1):
        pass_acts(hop)
        pass_bank(hop + 1)
        pass_rest(hop)
        own_next(hop)
    for hop in range(1, nz - 1):
        pass_next(hop, True)
    pass_acts(nz - 1)
    for d in range(1, nz - 1):
        gacc[...] += gather(d)
    pass_rest(nz - 1)
    half[...] = (gacc[...] + gather(nz - 1)).astype(BF16)

    for i in range(nz // 2):
        for e, r, c, s in plane:
            plane_copy(2 * i, e, s, (r, c)).wait_recv()
    for zs, valid in handed:
        @pl.when(valid)
        def _(zs=zs):
            own_copy(zs).wait()

    for i in (3, 4, 5):
        loads[i].wait()
    step = 256 if width % 256 == 0 else width
    right = as_matrix(rbuf[...])
    rotated = jnp.dot(half[...], right, preferred_element_type=F32)
    new_moment = 0.8 * mbuf[...] + 0.2 * rotated
    new_second = 0.9 * sbuf[...] + 0.1 * rotated * rotated
    scaled = (new_moment / (jnp.sqrt(new_second) + 1e-08)).astype(BF16)
    back[...] = jnp.dot(left, scaled, preferred_element_type=F32).astype(BF16)

    for n in range(0, width, step):
        cut = slice(n, n + step)
        full = lax.dot_general(
            back[...], right[cut, :], (((1,), (1,)), ((), ())), preferred_element_type=F32
        )
        update[:, cut] = full.astype(BF16)
        half[:, cut] = (wbuf[:, cut].astype(F32) - 0.001 * full).astype(BF16)

    for hop in range(1, nz):
        pass_next(hop, False)

    term = lax.dot_general(
        nfull[...].reshape(nz * 2 * ntok, width), half[...],
        (((1,), (1,)), ((), ())), preferred_element_type=F32,
    )
    terms[...] = term
    rsend[...] = term.astype(BF16).reshape(rsend.shape)
    for d, c in col_peers[::-1]:
        go(remote(rsend.at[c], rrecv.at[col], r_s.at[d], r_r.at[col], (row, c)))

    share = out.shape[0]
    total = terms[pl.ds(pl.multiple_of(col * share, share), share)]
    for d, c in col_peers:
        remote(rsend.at[c], rrecv.at[c], r_s.at[c], r_r.at[c], (row, c)).wait_recv()
        total = total + rrecv[c].astype(F32)
    out[...] = total.astype(BF16)

    for copy in sends:
        copy.wait_send()

    for cond, copy in guards:
        @pl.when(cond)
        def _(copy=copy):
            copy.wait_send()

    for zs, valid in handed:
        @pl.when(valid)
        def _(zs=zs):
            for e, r, c, _ in plane:
                plane_copy(zs, e, slot, (r, c)).wait_send()


def finish(update_in, out_in, update, out, sems):
    puts = [
        pltpu.make_async_copy(update_in, update, sems.at[0]),
        pltpu.make_async_copy(out_in, out, sems.at[1]),
    ]
    for put in puts:
        put.start()
    for put in puts:
        put.wait()


def per_device(
    acts, grads, next_acts, weight, moment, second, left_bank, right_bank, left_index, right_index,
    *, nr, nc,
):
    nz = nr // 2
    tok, width = acts.shape
    gtok, bo = grads.shape
    ntok = next_acts.shape[0]
    bank, rrows, _ = right_bank.shape
    lanes = width // 2
    share = nr * ntok // nc
    dma = pltpu.SemaphoreType.DMA
    anyspace = pl.BlockSpec(memory_space=pl.ANY)
    acts, grads, next_acts, weight, moment, second, left_bank, right_bank = [
        pltpu.with_memory_space_constraint(a, pltpu.HBM)
        for a in (acts, grads, next_acts, weight, moment, second, left_bank, right_bank)
    ]
    vmem = pl.BlockSpec(memory_space=pltpu.VMEM)
    update, out = pl.pallas_call(
        functools.partial(kernel, nz, nc),
        out_shape=(
            pltpu.VMEM(weight.shape, BF16),
            pltpu.VMEM((share, bo), BF16),
        ),
        in_specs=[anyspace] * 8 + [vmem] * 2,
        out_specs=(vmem, vmem),
        scratch_shapes=[
            pltpu.VMEM((nz, 2, tok, width), BF16),
            pltpu.VMEM((nc * gtok, bo), BF16),
            pltpu.VMEM((bo, nc * gtok), BF16),
            pltpu.VMEM((nz, 2, ntok, width), BF16),
            pltpu.VMEM(weight.shape, BF16),
            pltpu.VMEM(weight.shape, F32),
            pltpu.VMEM(weight.shape, F32),
            pltpu.VMEM(left_bank.shape, BF16),
            pltpu.VMEM((nz // 2, bank, rrows, lanes), BF16),
            pltpu.VMEM((nz // 2, 8, rrows, lanes), BF16),
            pltpu.VMEM((nz // 2, 2, 2, rrows, width), BF16),
            pltpu.VMEM((8, 128), jnp.int32),
            pltpu.VMEM((8, 8, 128), jnp.int32),
            pltpu.SMEM((8, 8, 128), jnp.int32),
            pltpu.VMEM(weight.shape, F32),
            pltpu.VMEM(weight.shape, BF16),
            pltpu.VMEM(weight.shape, BF16),
            pltpu.VMEM((nr * ntok, bo), F32),
            pltpu.VMEM((nc, share, bo), BF16),
            pltpu.VMEM((nc, share, bo), BF16),
            pltpu.VMEM(weight.shape, BF16),
            pltpu.VMEM((share, bo), BF16),
            dma((10,)),
            dma((nz + 2,)), dma((nz,)), dma((nz,)), dma((nz,)), dma((nz,)), dma((nz,)),
            dma((nz + 2,)), dma((nz,)), dma((1,)), dma((1,)),
            dma((nz + 2,)), dma((nz // 2,)),
            dma((nc,)), dma((nc,)),
            dma((8,)), dma((8,)), dma((nz // 2, 8)), dma((nz // 2, 8)), dma((nz // 2,)),
            dma((nc,)), dma((nc,)),
        ],
        compiler_params=pltpu.CompilerParams(
            collective_id=0, has_side_effects=True, vmem_limit_bytes=40 * 2**20,
        ),
    )(acts, grads, next_acts, weight, moment, second, left_bank, right_bank, left_index,
      right_index)
    update, out = [pltpu.with_memory_space_constraint(a, pltpu.VMEM) for a in (update, out)]
    return pl.pallas_call(
        finish,
        out_shape=(
            jax.ShapeDtypeStruct(weight.shape, BF16),
            jax.ShapeDtypeStruct((share, bo), BF16),
        ),
        in_specs=[vmem] * 2,
        out_specs=(anyspace, anyspace),
        scratch_shapes=[dma((2,))],
    )(update, out)


def solution(mesh):
    nr, nc = mesh.shape["row"], mesh.shape["col"]
    return jax.shard_map(
        functools.partial(per_device, nr=nr, nc=nc),
        mesh=mesh,
        in_specs=(
            P("row", "col"), P("col", "row"), P("row", "col"), P("row", "col"),
            P("row", "col"), P("row", "col"), P(), P(None, "row", None),
            P("row", "col"), P("row", "col"),
        ),
        out_specs=(P("row", "col"), P("col", "row")),
        check_vma=False,
    )
```

```python
import functools

import jax
import jax.numpy as jnp
from jax import lax
from jax.experimental import pallas as pl
from jax.experimental.pallas import tpu as pltpu
from jax.sharding import PartitionSpec as P

F32 = jnp.float32
BF16 = jnp.bfloat16
MESH = pl.DeviceIdType.MESH


def flip(value, bits, size):
    out, place = 0, 1
    while place < size:
        bit = (value // place) % 2
        out = out + place * ((1 - bit) if (bits // place) % 2 else bit)
        place *= 2
    return out


def as_matrix(value):
    cols = value.shape[-1]
    if value.shape[-2] % 16:
        return value.astype(F32).reshape(-1, cols).astype(BF16)
    return value.reshape(-1, cols)


def kernel(
    nz, nc,
    acts, grads, nxt, weight, moment, second, left_bank, right_bank, left_index, right_index,
    update, out,
    afull, gfull, gturn, nfull, wbuf, mbuf, sbuf, lbuf, bz, sel, rbuf,
    my_pick, picks, picks_smem, gacc, half, back, terms, rsend, rrecv, ubuf, obuf,
    local, a_s, a_r, ay_s, ay_r, ad_s, ad_r, n_s, n_r, ny_s, ny_r, b_s, b_r,
    g_s, g_r, p_s, p_r, s_s, s_r, own_s, r_s, r_r,
):
    row, col = lax.axis_index("row"), lax.axis_index("col")
    z, y = row // 2, row % 2
    quad, q = col // 4, col % 4
    x, k = q // 2, q % 2
    tok = acts.shape[0]
    ntok = nxt.shape[0]
    gtok = grads.shape[0]
    width = acts.shape[1]
    lanes = width // 2
    slot = y * 4 + q
    my_lanes = pl.ds(pl.multiple_of(x * lanes, 128), lanes)

    def remote(src, dst, ss, rs, device):
        return pltpu.make_async_remote_copy(
            src_ref=src, dst_ref=dst, send_sem=ss, recv_sem=rs,
            device_id=device, device_id_type=MESH,
        )

    plane = [
        (dy * 4 + dq, 2 * z + ((1 - y) if dy else y), quad * 4 + flip(q, dq, 4),
         ((1 - y) if dy else y) * 4 + flip(q, dq, 4))
        for dy in range(2) for dq in range(4) if dy or dq
    ]
    col_peers = [(d, flip(col, d, nc)) for d in range(1, nc)]
    far_cols = [peer for d, peer in col_peers if d >= 4]
    mate = (2 * z + 1 - y, col)
    up, down = (2 * (z + 1) + y, col), (2 * (z - 1) + y, col)
    has_up, has_down = z < nz - 1, z > 0
    holds = z % 2 == k

    loads = [
        (acts, afull.at[z, y]), (nxt, nfull.at[z, y]),
        (grads, gfull.at[pl.ds(pl.multiple_of(col * gtok, gtok), gtok)]),
        (weight, wbuf), (moment, mbuf), (second, sbuf), (left_bank, lbuf),
    ]
    loads = [pltpu.make_async_copy(s, d, local.at[i]) for i, (s, d) in enumerate(loads)]
    own_bank = pltpu.make_async_copy(
        right_bank.at[:, :, my_lanes], bz.at[z // 2], local.at[7]
    )

    barrier = pltpu.get_barrier_semaphore()
    friends = [(r, c) for _, r, c, _ in plane] + [(row, c) for c in far_cols]
    for friend in friends:
        pl.semaphore_signal(barrier, inc=1, device_id=friend, device_id_type=MESH)
    for there, friend in ((has_up, up), (has_down, down)):
        @pl.when(there)
        def _(friend=friend):
            pl.semaphore_signal(barrier, inc=1, device_id=friend, device_id_type=MESH)

    @pl.when(holds)
    def _():
        own_bank.start()

    for load in loads:
        load.start()

    head = lax.broadcasted_iota(jnp.int32, my_pick.shape, 0) == 0
    my_pick[...] = jnp.where(
        head, jnp.broadcast_to(right_index[...], my_pick.shape),
        jnp.broadcast_to(left_index[...], my_pick.shape),
    )
    picks[slot] = my_pick[...]
    pl.semaphore_wait(
        barrier, len(friends) + jnp.where(has_up, 1, 0) + jnp.where(has_down, 1, 0)
    )

    sends, guards, handed = [], [], []

    def go(copy):
        copy.start()
        sends.append(copy)

    def guarded(cond, copy):
        @pl.when(cond)
        def _():
            copy.start()

        guards.append((cond, copy))

    def take(valid, copy):
        @pl.when(valid)
        def _():
            copy.wait_recv()

    def bank_copy(src, zs, ss, device):
        return remote(src, bz.at[zs // 2], ss, b_r.at[zs // 2], device)

    def both_ways(make, mine):
        guarded(has_up & mine, make(0, up))
        guarded(has_down & mine, make(1, down))

    yes = z >= 0
    early = 2 * tok // 8

    def line(full, src, zs, ss, rs, to):
        return remote(src, full.at[zs, y], ss, rs.at[zs], to)

    def at_end(zs):
        return (zs == 0) | (zs == nz - 1)

    for e, r, c, _ in plane:
        go(remote(my_pick, picks.at[slot], p_s.at[e], p_r.at[slot], (r, c)))
    bank_src = right_bank.at[:, :, my_lanes]
    both_ways(lambda i, to: bank_copy(bank_src, z, b_s.at[nz + i], to), holds)
    both_ways(lambda i, to: line(afull, acts, z, a_s.at[nz + i], a_r, to), yes)
    go(remote(acts, afull.at[z, y], ay_s.at[z], ay_r.at[z], mate))
    go(remote(nxt, nfull.at[z, y], ny_s.at[z], ny_r.at[z], mate))
    for d, c in col_peers:
        go(remote(grads, gfull.at[pl.ds(pl.multiple_of(col * gtok, gtok), gtok)],
                  g_s.at[d], g_r.at[col], (row, c)))

    for e, r, c, s in plane:
        remote(my_pick, picks.at[s], p_s.at[e], p_r.at[s], (r, c)).wait_recv()
    to_smem = pltpu.make_async_copy(picks, picks_smem, local.at[8])
    to_smem.start()
    to_smem.wait()

    def place(zs, slot_from):
        ys, qs = slot_from // 4, slot_from % 4
        at = pl.ds(pl.multiple_of((qs // 2) * lanes, 128), lanes)
        return rbuf.at[zs // 2, qs % 2, ys, :, at]

    def plane_copy(zs, e, s, device):
        i = zs // 2
        return remote(sel.at[i, e], place(zs, s), s_s.at[i, e], s_r.at[i, s], device)

    def own_copy(zs):
        return pltpu.make_async_copy(sel.at[zs // 2, 0], place(zs, slot), own_s.at[zs // 2])

    def hand_out(zs, valid):
        @pl.when(valid)
        def _():
            for e, s, copy in [
                (e, s, plane_copy(zs, e, slot, (r, c))) for e, r, c, s in plane[::-1]
            ] + [(0, slot, own_copy(zs))]:
                pick = picks_smem[s, 0, 0]
                piece = bz[zs // 2, 0]
                for b in range(1, bz.shape[1]):
                    piece = jnp.where(pick == b, bz[zs // 2, b], piece)
                sel[zs // 2, e] = piece
                copy.start()

        handed.append((zs, valid))

    @pl.when(holds)
    def _():
        own_bank.wait()

    hand_out(z, holds)

    def arrivals(hop):
        return [
            (lax.rem(zs + nz, nz), valid, on, to)
            for zs, valid, on, to in ((z - hop, z >= hop, has_up, up),
                                      (z + hop, z + hop < nz, has_down, down))
        ]

    def pass_bank(hop):
        for zs, valid, on, to in arrivals(hop):
            valid = valid & (zs % 2 == k)
            copy = bank_copy(bz.at[zs // 2], zs, b_s.at[zs], to)
            take(valid, copy)
            if hop < nz - 1:
                guarded(valid & on, copy)
            hand_out(zs, valid)

    def across(zs, rows):
        piece = afull.at[zs, y, rows]
        return remote(piece, piece, ay_s.at[zs], ay_r.at[zs], mate)

    def pass_acts(hop):
        for zs, valid, on, to in arrivals(hop):
            copy = line(afull, afull.at[zs, y], zs, a_s.at[zs], a_r, to)
            take(valid, copy)
            if hop < nz - 1:
                guarded(valid & on, copy)
            guarded(valid & at_end(zs), across(zs, pl.ds(0, early)))
            guarded(valid & jnp.logical_not(at_end(zs)), across(zs, pl.ds(0, tok)))

    def rest_copy(zs, to):
        piece = afull.at[zs, 1 - y, pl.ds(early, tok - early)]
        return remote(piece, piece, ad_s.at[zs], ad_r.at[zs], to)

    def pass_rest(hop):
        for zs, valid, on, to in arrivals(hop):
            valid = valid & at_end(zs)
            copy = rest_copy(zs, to)
            take(valid, copy)
            if hop < nz - 1:
                guarded(valid & on, copy)

    def next_plane(zs, ss, to):
        return remote(nfull.at[zs], nfull.at[zs], ss, n_r.at[zs], to)

    def next_line(zs, ss, to):
        return remote(nfull.at[zs, y], nfull.at[zs, y], ss, n_r.at[zs], to)

    def next_across(zs, part):
        piece = nfull.at[zs, part]
        return remote(piece, piece, ny_s.at[zs], ny_r.at[zs], mate)

    def own_next(hop):
        inner = jnp.logical_not(at_end(z))
        guarded(inner & (z == hop), next_line(z, n_s.at[nz], up))
        guarded(inner & (z == nz - 1 - hop), next_line(z, n_s.at[nz + 1], down))

    def pass_next(hop, inner):
        for zs, valid, on, to in arrivals(hop):
            valid = valid & (on if inner else jnp.logical_not(on)) & jnp.logical_not(at_end(zs))
            copy = next_line(zs, n_s.at[zs], to)
            take(valid, copy)
            if inner:
                guarded(valid, copy)
            guarded(valid, next_across(zs, y))

    def pass_plane(hop, inner):
        for zs, valid, on, to in arrivals(hop):
            valid = valid & (on if inner else jnp.logical_not(on)) & at_end(zs)
            copy = next_plane(zs, n_s.at[zs], to)
            take(valid, copy)
            if inner and hop < nz - 1:
                guarded(valid, copy)

    def take_acts(zs, rows):
        piece = afull.at[zs, 1 - y, rows]
        remote(piece, piece, ay_s.at[0], ay_r.at[zs], mate).wait_recv()

    def gather(d):
        zs = flip(z, d, nz) if d else z
        if d:
            @pl.when(at_end(zs))
            def _():
                take_acts(zs, pl.ds(0, early))

            @pl.when(jnp.logical_not(at_end(zs)))
            def _():
                take_acts(zs, pl.ds(0, tok))
        return jnp.dot(
            gturn[:, pl.ds(pl.multiple_of(zs * 2 * tok, 2 * tok), 2 * tok)],
            afull[zs].reshape(2 * tok, width), preferred_element_type=F32,
        )

    pass_bank(1)
    take_acts(z, pl.ds(0, tok))
    guarded(z == 0, rest_copy(z, up))
    guarded(z == nz - 1, rest_copy(z, down))
    loads[1].wait()
    next_across(z, 1 - y).wait_recv()
    guarded(z == 0, next_plane(z, n_s.at[nz], up))
    guarded(z == nz - 1, next_plane(z, n_s.at[nz + 1], down))
    pass_acts(1)
    if nz > 2:
        pass_bank(2)
        own_next(1)
        pass_rest(1)

    for i in (0, 2, 6):
        loads[i].wait()
    left_at = picks_smem[slot, 1, 0]
    left = lbuf[left_at]
    for d, c in col_peers:
        remote(grads, gfull.at[pl.ds(pl.multiple_of(c * gtok, gtok), gtok)],
               g_s.at[d], g_r.at[c], (row, c)).wait_recv()
    gturn[...] = lax.dot_general(
        left, gfull[...], (((0,), (1,)), ((), ())), preferred_element_type=F32
    ).astype(BF16)

    gacc[...] = gather(0)
    for hop in range(2, nz - 1):
        pass_acts(hop)
        pass_bank(hop + 1)
        own_next(hop)
        if hop == nz - 2:
            for on in range(1, nz - 1):
                pass_next(on, True)
        pass_rest(hop)
    for hop in range(1, nz - 1):
        pass_plane(hop, True)
    pass_acts(nz - 1)
    for hop in range(1, nz - 1):
        pass_next(hop, False)
    for d in range(1, nz - 1):
        gacc[...] += gather(d)
    pass_rest(nz - 1)
    half[...] = (gacc[...] + gather(nz - 1)).astype(BF16)

    for i in range(nz // 2):
        for e, r, c, s in plane:
            plane_copy(2 * i, e, s, (r, c)).wait_recv()
    for zs, valid in handed:
        @pl.when(valid)
        def _(zs=zs):
            own_copy(zs).wait()

    for i in (3, 4, 5):
        loads[i].wait()
    step = 256 if width % 256 == 0 else width
    right = as_matrix(rbuf[...])
    rotated = jnp.dot(half[...], right, preferred_element_type=F32)
    new_moment = 0.8 * mbuf[...] + 0.2 * rotated
    new_second = 0.9 * sbuf[...] + 0.1 * rotated * rotated
    scaled = (new_moment / (jnp.sqrt(new_second) + 1e-08)).astype(BF16)
    back[...] = jnp.dot(left, scaled, preferred_element_type=F32).astype(BF16)

    for n in range(0, width, step):
        cut = slice(n, n + step)
        full = lax.dot_general(
            back[...], right[cut, :], (((1,), (1,)), ((), ())), preferred_element_type=F32
        )
        update[:, cut] = full.astype(BF16)
        half[:, cut] = (wbuf[:, cut].astype(F32) - 0.001 * full).astype(BF16)

    for hop in range(1, nz):
        pass_plane(hop, False)
    for zs in range(1, nz - 1):
        @pl.when(z != zs)
        def _(zs=zs):
            next_across(zs, 1 - y).wait_recv()


    term = lax.dot_general(
        nfull[...].reshape(nz * 2 * ntok, width), half[...],
        (((1,), (1,)), ((), ())), preferred_element_type=F32,
    )
    terms[...] = term
    rsend[...] = term.astype(BF16).reshape(rsend.shape)
    for d, c in col_peers[::-1]:
        go(remote(rsend.at[c], rrecv.at[col], r_s.at[d], r_r.at[col], (row, c)))

    share = out.shape[0]
    total = terms[pl.ds(pl.multiple_of(col * share, share), share)]
    for d, c in col_peers:
        remote(rsend.at[c], rrecv.at[c], r_s.at[c], r_r.at[c], (row, c)).wait_recv()
        total = total + rrecv[c].astype(F32)
    out[...] = total.astype(BF16)

    for copy in sends:
        copy.wait_send()

    for cond, copy in guards:
        @pl.when(cond)
        def _(copy=copy):
            copy.wait_send()

    for zs, valid in handed:
        @pl.when(valid)
        def _(zs=zs):
            for e, r, c, _ in plane:
                plane_copy(zs, e, slot, (r, c)).wait_send()


def finish(update_in, out_in, update, out, sems):
    puts = [
        pltpu.make_async_copy(update_in, update, sems.at[0]),
        pltpu.make_async_copy(out_in, out, sems.at[1]),
    ]
    for put in puts:
        put.start()
    for put in puts:
        put.wait()


def per_device(
    acts, grads, next_acts, weight, moment, second, left_bank, right_bank, left_index, right_index,
    *, nr, nc,
):
    nz = nr // 2
    tok, width = acts.shape
    gtok, bo = grads.shape
    ntok = next_acts.shape[0]
    bank, rrows, _ = right_bank.shape
    lanes = width // 2
    share = nr * ntok // nc
    dma = pltpu.SemaphoreType.DMA
    anyspace = pl.BlockSpec(memory_space=pl.ANY)
    acts, grads, next_acts, weight, moment, second, left_bank, right_bank = [
        pltpu.with_memory_space_constraint(a, pltpu.HBM)
        for a in (acts, grads, next_acts, weight, moment, second, left_bank, right_bank)
    ]
    vmem = pl.BlockSpec(memory_space=pltpu.VMEM)
    update, out = pl.pallas_call(
        functools.partial(kernel, nz, nc),
        out_shape=(
            pltpu.VMEM(weight.shape, BF16),
            pltpu.VMEM((share, bo), BF16),
        ),
        in_specs=[anyspace] * 8 + [vmem] * 2,
        out_specs=(vmem, vmem),
        scratch_shapes=[
            pltpu.VMEM((nz, 2, tok, width), BF16),
            pltpu.VMEM((nc * gtok, bo), BF16),
            pltpu.VMEM((bo, nc * gtok), BF16),
            pltpu.VMEM((nz, 2, ntok, width), BF16),
            pltpu.VMEM(weight.shape, BF16),
            pltpu.VMEM(weight.shape, F32),
            pltpu.VMEM(weight.shape, F32),
            pltpu.VMEM(left_bank.shape, BF16),
            pltpu.VMEM((nz // 2, bank, rrows, lanes), BF16),
            pltpu.VMEM((nz // 2, 8, rrows, lanes), BF16),
            pltpu.VMEM((nz // 2, 2, 2, rrows, width), BF16),
            pltpu.VMEM((8, 128), jnp.int32),
            pltpu.VMEM((8, 8, 128), jnp.int32),
            pltpu.SMEM((8, 8, 128), jnp.int32),
            pltpu.VMEM(weight.shape, F32),
            pltpu.VMEM(weight.shape, BF16),
            pltpu.VMEM(weight.shape, BF16),
            pltpu.VMEM((nr * ntok, bo), F32),
            pltpu.VMEM((nc, share, bo), BF16),
            pltpu.VMEM((nc, share, bo), BF16),
            pltpu.VMEM(weight.shape, BF16),
            pltpu.VMEM((share, bo), BF16),
            dma((10,)),
            dma((nz + 2,)), dma((nz,)), dma((nz,)), dma((nz,)), dma((nz,)), dma((nz,)),
            dma((nz + 2,)), dma((nz,)), dma((nz,)), dma((nz,)),
            dma((nz + 2,)), dma((nz // 2,)),
            dma((nc,)), dma((nc,)),
            dma((8,)), dma((8,)), dma((nz // 2, 8)), dma((nz // 2, 8)), dma((nz // 2,)),
            dma((nc,)), dma((nc,)),
        ],
        compiler_params=pltpu.CompilerParams(
            collective_id=0, has_side_effects=True, vmem_limit_bytes=40 * 2**20,
        ),
    )(acts, grads, next_acts, weight, moment, second, left_bank, right_bank, left_index,
      right_index)
    update, out = [pltpu.with_memory_space_constraint(a, pltpu.VMEM) for a in (update, out)]
    return pl.pallas_call(
        finish,
        out_shape=(
            jax.ShapeDtypeStruct(weight.shape, BF16),
            jax.ShapeDtypeStruct((share, bo), BF16),
        ),
        in_specs=[vmem] * 2,
        out_specs=(anyspace, anyspace),
        scratch_shapes=[dma((2,))],
    )(update, out)


def solution(mesh):
    nr, nc = mesh.shape["row"], mesh.shape["col"]
    return jax.shard_map(
        functools.partial(per_device, nr=nr, nc=nc),
        mesh=mesh,
        in_specs=(
            P("row", "col"), P("col", "row"), P("row", "col"), P("row", "col"),
            P("row", "col"), P("row", "col"), P(), P(None, "row", None),
            P("row", "col"), P("row", "col"),
        ),
        out_specs=(P("row", "col"), P("col", "row")),
        check_vma=False,
    )
```

```python
import functools

import jax
import jax.numpy as jnp
from jax import lax
from jax.experimental import pallas as pl
from jax.experimental.pallas import tpu as pltpu
from jax.sharding import PartitionSpec as P

F32 = jnp.float32
BF16 = jnp.bfloat16
MESH = pl.DeviceIdType.MESH


def flip(value, bits, size):
    out, place = 0, 1
    while place < size:
        bit = (value // place) % 2
        out = out + place * ((1 - bit) if (bits // place) % 2 else bit)
        place *= 2
    return out


def as_matrix(value):
    cols = value.shape[-1]
    if value.shape[-2] % 16:
        return value.astype(F32).reshape(-1, cols).astype(BF16)
    return value.reshape(-1, cols)


def kernel(
    nz, nc,
    acts, grads, nxt, weight, moment, second, left_bank, right_bank, left_index, right_index,
    update, out,
    afull, gfull, gturn, nfull, wbuf, mbuf, sbuf, lbuf, bz, sel, rbuf,
    my_pick, picks, picks_smem, gacc, half, back, terms, rsend, rrecv, ubuf, obuf,
    local, a_s, a_r, ay_s, ay_r, ad_s, ad_r, n_s, n_r, ny_s, ny_r, b_s, b_r,
    g_s, g_r, p_s, p_r, s_s, s_r, own_s, r_s, r_r,
):
    row, col = lax.axis_index("row"), lax.axis_index("col")
    z, y = row // 2, row % 2
    quad, q = col // 4, col % 4
    x, k = q // 2, q % 2
    tok = acts.shape[0]
    ntok = nxt.shape[0]
    gtok = grads.shape[0]
    width = acts.shape[1]
    lanes = width // 2
    slot = y * 4 + q
    my_lanes = pl.ds(pl.multiple_of(x * lanes, 128), lanes)

    def remote(src, dst, ss, rs, device):
        return pltpu.make_async_remote_copy(
            src_ref=src, dst_ref=dst, send_sem=ss, recv_sem=rs,
            device_id=device, device_id_type=MESH,
        )

    plane = [
        (dy * 4 + dq, 2 * z + ((1 - y) if dy else y), quad * 4 + flip(q, dq, 4),
         ((1 - y) if dy else y) * 4 + flip(q, dq, 4))
        for dy in range(2) for dq in range(4) if dy or dq
    ]
    col_peers = [(d, flip(col, d, nc)) for d in range(1, nc)]
    far_cols = [peer for d, peer in col_peers if d >= 4]
    mate = (2 * z + 1 - y, col)
    up, down = (2 * (z + 1) + y, col), (2 * (z - 1) + y, col)
    has_up, has_down = z < nz - 1, z > 0
    holds = z % 2 == k

    loads = [
        (acts, afull.at[z, y]), (nxt, nfull.at[z, y]),
        (grads, gfull.at[pl.ds(pl.multiple_of(col * gtok, gtok), gtok)]),
        (weight, wbuf), (moment, mbuf), (second, sbuf), (left_bank, lbuf),
    ]
    loads = [pltpu.make_async_copy(s, d, local.at[i]) for i, (s, d) in enumerate(loads)]
    own_bank = pltpu.make_async_copy(
        right_bank.at[:, :, my_lanes], bz.at[z // 2], local.at[7]
    )

    barrier = pltpu.get_barrier_semaphore()
    friends = [(r, c) for _, r, c, _ in plane] + [(row, c) for c in far_cols]
    for friend in friends:
        pl.semaphore_signal(barrier, inc=1, device_id=friend, device_id_type=MESH)
    for there, friend in ((has_up, up), (has_down, down)):
        @pl.when(there)
        def _(friend=friend):
            pl.semaphore_signal(barrier, inc=1, device_id=friend, device_id_type=MESH)

    @pl.when(holds)
    def _():
        own_bank.start()

    for load in loads:
        load.start()

    head = lax.broadcasted_iota(jnp.int32, my_pick.shape, 0) == 0
    my_pick[...] = jnp.where(
        head, jnp.broadcast_to(right_index[...], my_pick.shape),
        jnp.broadcast_to(left_index[...], my_pick.shape),
    )
    picks[slot] = my_pick[...]
    pl.semaphore_wait(
        barrier, len(friends) + jnp.where(has_up, 1, 0) + jnp.where(has_down, 1, 0)
    )

    sends, guards, handed = [], [], []

    def go(copy):
        copy.start()
        sends.append(copy)

    def guarded(cond, copy):
        @pl.when(cond)
        def _():
            copy.start()

        guards.append((cond, copy))

    def take(valid, copy):
        @pl.when(valid)
        def _():
            copy.wait_recv()

    def bank_copy(src, zs, ss, device):
        return remote(src, bz.at[zs // 2], ss, b_r.at[zs // 2], device)

    def both_ways(make, mine):
        guarded(has_up & mine, make(0, up))
        guarded(has_down & mine, make(1, down))

    yes = z >= 0
    early = 2 * tok // 8

    def line(full, src, zs, ss, rs, to):
        return remote(src, full.at[zs, y], ss, rs.at[zs], to)

    def at_end(zs):
        return (zs == 0) | (zs == nz - 1)

    for e, r, c, _ in plane:
        go(remote(my_pick, picks.at[slot], p_s.at[e], p_r.at[slot], (r, c)))
    bank_src = right_bank.at[:, :, my_lanes]
    both_ways(lambda i, to: bank_copy(bank_src, z, b_s.at[nz + i], to), holds)
    both_ways(lambda i, to: line(afull, acts, z, a_s.at[nz + i], a_r, to), yes)
    go(remote(nxt, nfull.at[z, y], ny_s.at[z], ny_r.at[z], mate))
    go(remote(acts, afull.at[z, y], ay_s.at[z], ay_r.at[z], mate))
    for d, c in col_peers:
        go(remote(grads, gfull.at[pl.ds(pl.multiple_of(col * gtok, gtok), gtok)],
                  g_s.at[d], g_r.at[col], (row, c)))

    for e, r, c, s in plane:
        remote(my_pick, picks.at[s], p_s.at[e], p_r.at[s], (r, c)).wait_recv()
    to_smem = pltpu.make_async_copy(picks, picks_smem, local.at[8])
    to_smem.start()
    to_smem.wait()

    def place(zs, slot_from):
        ys, qs = slot_from // 4, slot_from % 4
        at = pl.ds(pl.multiple_of((qs // 2) * lanes, 128), lanes)
        return rbuf.at[zs // 2, qs % 2, ys, :, at]

    def plane_copy(zs, e, s, device):
        i = zs // 2
        return remote(sel.at[i, e], place(zs, s), s_s.at[i, e], s_r.at[i, s], device)

    def own_copy(zs):
        return pltpu.make_async_copy(sel.at[zs // 2, 0], place(zs, slot), own_s.at[zs // 2])

    def hand_out(zs, valid):
        @pl.when(valid)
        def _():
            for e, s, copy in [
                (e, s, plane_copy(zs, e, slot, (r, c))) for e, r, c, s in plane[::-1]
            ] + [(0, slot, own_copy(zs))]:
                pick = picks_smem[s, 0, 0]
                piece = bz[zs // 2, 0]
                for b in range(1, bz.shape[1]):
                    piece = jnp.where(pick == b, bz[zs // 2, b], piece)
                sel[zs // 2, e] = piece
                copy.start()

        handed.append((zs, valid))

    @pl.when(holds)
    def _():
        own_bank.wait()

    hand_out(z, holds)

    def arrivals(hop):
        return [
            (lax.rem(zs + nz, nz), valid, on, to)
            for zs, valid, on, to in ((z - hop, z >= hop, has_up, up),
                                      (z + hop, z + hop < nz, has_down, down))
        ]

    def pass_bank(hop):
        for zs, valid, on, to in arrivals(hop):
            valid = valid & (zs % 2 == k)
            copy = bank_copy(bz.at[zs // 2], zs, b_s.at[zs], to)
            take(valid, copy)
            if hop < nz - 1:
                guarded(valid & on, copy)
            hand_out(zs, valid)

    def across(zs, rows):
        piece = afull.at[zs, y, rows]
        return remote(piece, piece, ay_s.at[zs], ay_r.at[zs], mate)

    def pass_acts(hop):
        for zs, valid, on, to in arrivals(hop):
            copy = line(afull, afull.at[zs, y], zs, a_s.at[zs], a_r, to)
            take(valid, copy)
            if hop < nz - 1:
                guarded(valid & on, copy)
            guarded(valid & at_end(zs), across(zs, pl.ds(0, early)))
            guarded(valid & jnp.logical_not(at_end(zs)), across(zs, pl.ds(0, tok)))

    def rest_copy(zs, to):
        piece = afull.at[zs, 1 - y, pl.ds(early, tok - early)]
        return remote(piece, piece, ad_s.at[zs], ad_r.at[zs], to)

    def pass_rest(hop):
        for zs, valid, on, to in arrivals(hop):
            valid = valid & at_end(zs)
            copy = rest_copy(zs, to)
            take(valid, copy)
            if hop < nz - 1:
                guarded(valid & on, copy)

    def next_plane(zs, ss, to):
        return remote(nfull.at[zs], nfull.at[zs], ss, n_r.at[zs], to)

    def next_line(zs, ss, to):
        return remote(nfull.at[zs, y], nfull.at[zs, y], ss, n_r.at[zs], to)

    def next_across(zs, part):
        piece = nfull.at[zs, part]
        return remote(piece, piece, ny_s.at[zs], ny_r.at[zs], mate)

    def own_next(hop):
        inner = jnp.logical_not(at_end(z))
        guarded(inner & (z == hop), next_line(z, n_s.at[nz], up))
        guarded(inner & (z == nz - 1 - hop), next_line(z, n_s.at[nz + 1], down))

    def pass_next(hop, inner):
        for zs, valid, on, to in arrivals(hop):
            valid = valid & (on if inner else jnp.logical_not(on)) & jnp.logical_not(at_end(zs))
            copy = next_line(zs, n_s.at[zs], to)
            take(valid, copy)
            if inner:
                guarded(valid, copy)
            guarded(valid, next_across(zs, y))

    def pass_plane(hop, inner):
        for zs, valid, on, to in arrivals(hop):
            valid = valid & (on if inner else jnp.logical_not(on)) & at_end(zs)
            copy = next_plane(zs, n_s.at[zs], to)
            take(valid, copy)
            if inner and hop < nz - 1:
                guarded(valid, copy)

    def take_acts(zs, rows):
        piece = afull.at[zs, 1 - y, rows]
        remote(piece, piece, ay_s.at[0], ay_r.at[zs], mate).wait_recv()

    def gather(d):
        zs = flip(z, d, nz) if d else z
        if d:
            @pl.when(at_end(zs))
            def _():
                take_acts(zs, pl.ds(0, early))

            @pl.when(jnp.logical_not(at_end(zs)))
            def _():
                take_acts(zs, pl.ds(0, tok))
        return jnp.dot(
            gturn[:, pl.ds(pl.multiple_of(zs * 2 * tok, 2 * tok), 2 * tok)],
            afull[zs].reshape(2 * tok, width), preferred_element_type=F32,
        )

    pass_bank(1)
    take_acts(z, pl.ds(0, tok))
    guarded(z == 0, rest_copy(z, up))
    guarded(z == nz - 1, rest_copy(z, down))
    loads[1].wait()
    next_across(z, 1 - y).wait_recv()
    guarded(z == 0, next_plane(z, n_s.at[nz], up))
    guarded(z == nz - 1, next_plane(z, n_s.at[nz + 1], down))
    pass_acts(1)
    if nz > 2:
        pass_bank(2)
        own_next(1)
        pass_rest(1)

    for i in (0, 2, 6):
        loads[i].wait()
    left_at = picks_smem[slot, 1, 0]
    left = lbuf[left_at]
    for d, c in col_peers:
        remote(grads, gfull.at[pl.ds(pl.multiple_of(c * gtok, gtok), gtok)],
               g_s.at[d], g_r.at[c], (row, c)).wait_recv()
    gturn[...] = lax.dot_general(
        left, gfull[...], (((0,), (1,)), ((), ())), preferred_element_type=F32
    ).astype(BF16)

    gacc[...] = gather(0)
    for hop in range(2, nz - 1):
        pass_acts(hop)
        pass_bank(hop + 1)
        own_next(hop)
        if hop == nz - 2:
            for on in range(1, nz - 1):
                pass_next(on, True)
        pass_rest(hop)
    for hop in range(1, nz - 1):
        pass_plane(hop, True)
    pass_acts(nz - 1)
    for hop in range(1, nz - 1):
        pass_next(hop, False)
    for d in range(1, nz - 1):
        gacc[...] += gather(d)
    pass_rest(nz - 1)
    half[...] = (gacc[...] + gather(nz - 1)).astype(BF16)

    for i in range(nz // 2):
        for e, r, c, s in plane:
            plane_copy(2 * i, e, s, (r, c)).wait_recv()
    for zs, valid in handed:
        @pl.when(valid)
        def _(zs=zs):
            own_copy(zs).wait()

    for i in (3, 4, 5):
        loads[i].wait()
    step = 256 if width % 256 == 0 else width
    right = as_matrix(rbuf[...])
    rotated = jnp.dot(half[...], right, preferred_element_type=F32)
    new_moment = 0.8 * mbuf[...] + 0.2 * rotated
    new_second = 0.9 * sbuf[...] + 0.1 * rotated * rotated
    scaled = (new_moment / (jnp.sqrt(new_second) + 1e-08)).astype(BF16)
    back[...] = jnp.dot(left, scaled, preferred_element_type=F32).astype(BF16)

    for hop in range(1, nz):
        pass_plane(hop, False)
    for zs in range(1, nz - 1):
        @pl.when(z != zs)
        def _(zs=zs):
            next_across(zs, 1 - y).wait_recv()


    tokens = nfull[...].reshape(nz * 2 * ntok, width)
    term = None
    for n in range(0, width, step):
        cut = slice(n, n + step)
        full = lax.dot_general(
            back[...], right[cut, :], (((1,), (1,)), ((), ())), preferred_element_type=F32
        )
        update[:, cut] = full.astype(BF16)
        half[:, cut] = (wbuf[:, cut].astype(F32) - 0.001 * full).astype(BF16)
        product = lax.dot_general(
            tokens[:, cut], half[:, cut], (((1,), (1,)), ((), ())), preferred_element_type=F32
        )
        term = product if term is None else term + product
    terms[...] = term
    rsend[...] = term.astype(BF16).reshape(rsend.shape)
    for d, c in col_peers[::-1]:
        go(remote(rsend.at[c], rrecv.at[col], r_s.at[d], r_r.at[col], (row, c)))

    share = out.shape[0]
    total = terms[pl.ds(pl.multiple_of(col * share, share), share)]
    for d, c in col_peers:
        remote(rsend.at[c], rrecv.at[c], r_s.at[c], r_r.at[c], (row, c)).wait_recv()
        total = total + rrecv[c].astype(F32)
    out[...] = total.astype(BF16)

    for copy in sends:
        copy.wait_send()

    for cond, copy in guards:
        @pl.when(cond)
        def _(copy=copy):
            copy.wait_send()

    for zs, valid in handed:
        @pl.when(valid)
        def _(zs=zs):
            for e, r, c, _ in plane:
                plane_copy(zs, e, slot, (r, c)).wait_send()


def finish(update_in, out_in, update, out, sems):
    puts = [
        pltpu.make_async_copy(update_in, update, sems.at[0]),
        pltpu.make_async_copy(out_in, out, sems.at[1]),
    ]
    for put in puts:
        put.start()
    for put in puts:
        put.wait()


def per_device(
    acts, grads, next_acts, weight, moment, second, left_bank, right_bank, left_index, right_index,
    *, nr, nc,
):
    nz = nr // 2
    tok, width = acts.shape
    gtok, bo = grads.shape
    ntok = next_acts.shape[0]
    bank, rrows, _ = right_bank.shape
    lanes = width // 2
    share = nr * ntok // nc
    dma = pltpu.SemaphoreType.DMA
    anyspace = pl.BlockSpec(memory_space=pl.ANY)
    acts, grads, next_acts, weight, moment, second, left_bank, right_bank = [
        pltpu.with_memory_space_constraint(a, pltpu.HBM)
        for a in (acts, grads, next_acts, weight, moment, second, left_bank, right_bank)
    ]
    vmem = pl.BlockSpec(memory_space=pltpu.VMEM)
    update, out = pl.pallas_call(
        functools.partial(kernel, nz, nc),
        out_shape=(
            pltpu.VMEM(weight.shape, BF16),
            pltpu.VMEM((share, bo), BF16),
        ),
        in_specs=[anyspace] * 8 + [vmem] * 2,
        out_specs=(vmem, vmem),
        scratch_shapes=[
            pltpu.VMEM((nz, 2, tok, width), BF16),
            pltpu.VMEM((nc * gtok, bo), BF16),
            pltpu.VMEM((bo, nc * gtok), BF16),
            pltpu.VMEM((nz, 2, ntok, width), BF16),
            pltpu.VMEM(weight.shape, BF16),
            pltpu.VMEM(weight.shape, F32),
            pltpu.VMEM(weight.shape, F32),
            pltpu.VMEM(left_bank.shape, BF16),
            pltpu.VMEM((nz // 2, bank, rrows, lanes), BF16),
            pltpu.VMEM((nz // 2, 8, rrows, lanes), BF16),
            pltpu.VMEM((nz // 2, 2, 2, rrows, width), BF16),
            pltpu.VMEM((8, 128), jnp.int32),
            pltpu.VMEM((8, 8, 128), jnp.int32),
            pltpu.SMEM((8, 8, 128), jnp.int32),
            pltpu.VMEM(weight.shape, F32),
            pltpu.VMEM(weight.shape, BF16),
            pltpu.VMEM(weight.shape, BF16),
            pltpu.VMEM((nr * ntok, bo), F32),
            pltpu.VMEM((nc, share, bo), BF16),
            pltpu.VMEM((nc, share, bo), BF16),
            pltpu.VMEM(weight.shape, BF16),
            pltpu.VMEM((share, bo), BF16),
            dma((10,)),
            dma((nz + 2,)), dma((nz,)), dma((nz,)), dma((nz,)), dma((nz,)), dma((nz,)),
            dma((nz + 2,)), dma((nz,)), dma((nz,)), dma((nz,)),
            dma((nz + 2,)), dma((nz // 2,)),
            dma((nc,)), dma((nc,)),
            dma((8,)), dma((8,)), dma((nz // 2, 8)), dma((nz // 2, 8)), dma((nz // 2,)),
            dma((nc,)), dma((nc,)),
        ],
        compiler_params=pltpu.CompilerParams(
            collective_id=0, has_side_effects=True, vmem_limit_bytes=40 * 2**20,
        ),
    )(acts, grads, next_acts, weight, moment, second, left_bank, right_bank, left_index,
      right_index)
    update, out = [pltpu.with_memory_space_constraint(a, pltpu.VMEM) for a in (update, out)]
    return pl.pallas_call(
        finish,
        out_shape=(
            jax.ShapeDtypeStruct(weight.shape, BF16),
            jax.ShapeDtypeStruct((share, bo), BF16),
        ),
        in_specs=[vmem] * 2,
        out_specs=(anyspace, anyspace),
        scratch_shapes=[dma((2,))],
    )(update, out)


def solution(mesh):
    nr, nc = mesh.shape["row"], mesh.shape["col"]
    return jax.shard_map(
        functools.partial(per_device, nr=nr, nc=nc),
        mesh=mesh,
        in_specs=(
            P("row", "col"), P("col", "row"), P("row", "col"), P("row", "col"),
            P("row", "col"), P("row", "col"), P(), P(None, "row", None),
            P("row", "col"), P("row", "col"),
        ),
        out_specs=(P("row", "col"), P("col", "row")),
        check_vma=False,
    )
```
